512 devices in a mesh: ctx: 64 (over y_hi, x, z), exp: 8 (over y_lo, core).
Axes of the slice: x: 4, y: 8 (y_hi: 2, y_lo: 4; y = y_hi * 4 + y_lo), z: 8, core: 2. Of those that a mesh axis runs over, the one named last changes fastest.
Arguments:
- queries: bfloat16 [4096, 6144], P('ctx', 'exp'), may hold values from -5 to 5
- keys: bfloat16 [4096, 1024], P('ctx', 'exp'), may hold values from -5 to 5
- values: bfloat16 [4096, 1024], P('ctx', 'exp'), may hold values from -16 to 16
- residual: bfloat16 [4096, 6144], P('ctx', 'exp'), may hold values from -25 to 25
- norm_gain: float32 [6144], P('exp'), may hold values from 0.5 to 1.5
- routes: int32 [4096, 1], P('ctx'), may hold values from 0 to 3; in each aligned block of 64 rows (0 to 63, 64 to 127, ...) at most 24 rows name the same one
- route_weight: float32 [4096], P('ctx'), may hold values from 0.25 to 1
- w_gate: bfloat16 [65536, 6144], P('ctx', 'exp'), may hold values from -0.078125 to 0.078125
- w_up: bfloat16 [65536, 6144], P('ctx', 'exp'), may hold values from -0.078125 to 0.078125
- w_down: bfloat16 [65536, 6144], P('ctx', 'exp'), may hold values from -0.046875 to 0.046875
Outputs:
- moe_out: bfloat16 [4096, 6144], P('ctx', 'exp')
The draws below stay inside these ranges and needn't reach their ends.
Inputs may be any that keep to these rules, and one draw needn't show every extreme that they name: `routes`: within the 64 rows of one device, at most 24 tokens have the same route.
All inputs are finite; a program needn't handle non-finite values.
Results may differ from the reference program's by a relative error of at most 0.029.
Values may be sent and summed in bfloat16 or wider, within the bound.
No kernel may reach another device: no remote copies, remote signals or barrier semaphores. Data moves between devices by JAX's collectives and lax.ppermute only.
A program may use at most 64 MiB of HBM per device.

```python
import math
import jax
import jax.numpy as jnp
import numpy as np
from jax import lax

D = 6144
H = 48
KV_HEADS = 8
HD = 128
FF = 16384
EXPERTS = 4
TOK_DEV = 64
TOKENS = 4096
CAP = 24
N_CTX = 64
N_EXP = 8


def draw_queries(key, part):
    row_width = H * HD
    result = jnp.clip(jax.random.normal(jax.random.fold_in(key, 1), (TOKENS, row_width), jnp.float32), -5.0, 5.0)
    return result.astype(jnp.bfloat16)


def draw_keys(key, part):
    row_width = KV_HEADS * HD
    result = jnp.clip(jax.random.normal(jax.random.fold_in(key, 2), (TOKENS, row_width), jnp.float32), -5.0, 5.0)
    return result.astype(jnp.bfloat16)


def draw_residual(key, part):
    column_pos = jnp.arange(D).astype(jnp.float32) / D
    col_scale = 10.0 ** jax.random.uniform(jax.random.fold_in(key, 3), (D,), jnp.float32) * 3.0 ** column_pos
    row_scale = 10.0 ** jax.random.uniform(jax.random.fold_in(key, 4), (TOKENS,), jnp.float32)
    noise_draw = jnp.clip(jax.random.normal(jax.random.fold_in(key, 5), (TOKENS, D), jnp.float32), -4.0, 4.0)
    result = 0.01 * noise_draw * row_scale[:, None] * col_scale[None, :]
    return result.astype(jnp.bfloat16)


def levels(rng, dims, pieces, low, largest):
    gain, own = 1.0, jax.random.fold_in(rng, 6)
    for dim, shards_of in pieces:
        heights = jnp.exp(jax.random.uniform(jax.random.fold_in(own, dim), (shards_of,), jnp.float32, low / len(pieces), largest / len(pieces)))
        gain = gain * jnp.repeat(heights, dims[dim] // shards_of).reshape([-1 if axis == dim else 1 for axis in range(len(dims))])
    return gain


def assign_block(key, own, number, rows, count, top, most, lean):
    ranking = jax.random.permutation(key, count)
    crowded, usual = load_shares(count, rows * top, most, lean, True), load_shares(count, rows * top, most, lean, False)
    places = jnp.arange(count)

    def named(tallies, turn):
        used = int((tallies > 0).sum())
        fixed = max(1, used // 4)
        passed = fixed + (places - fixed + turn * (used - fixed)) % max(1, count - fixed)
        return jnp.zeros((count,), jnp.int32).at[ranking[jnp.where(places < fixed, places, passed)]].set(jnp.asarray(tallies, jnp.int32))

    tallies = jnp.where(number % 4 == 0, named(crowded, number // 4), named(usual, number - number // 4 - 1))
    mixed = jax.random.permutation(jax.random.fold_in(own, 3), count)
    source_of, sink = mixed[0:count // 2 * 2:2], mixed[1:count // 2 * 2:2]
    slack = jnp.minimum(tallies[source_of] - 1, most - tallies[sink]) // 2
    slack = jnp.where((source_of == ranking[0]) | (sink == ranking[0]) | (tallies[sink] == 0), 0, jnp.maximum(slack, 0))
    passed = jax.random.randint(jax.random.fold_in(own, 4), (count // 2,), 0, 1 << 20) % (slack + 1)
    tallies = tallies.at[source_of].add(-passed).at[sink].add(passed)
    labels = jnp.searchsorted(jnp.cumsum(tallies), jnp.arange(rows * top), side="right").astype(jnp.int32)
    listing = labels.reshape(top, rows).T
    listing = listing[jax.random.permutation(jax.random.fold_in(own, 1), rows)]
    turn = jax.random.randint(jax.random.fold_in(own, 2), (rows, 1), 0, top)
    return jnp.take_along_axis(listing, (jnp.arange(top)[None, :] + turn) % top, axis=1)


def load_shares(number_of, total, most, skew, full):
    portions = [(1 << 20) // math.isqrt(grade ** skew) + 1 for grade in range(1, number_of + 1)]
    largest = most if full else min(most, max(-(-total // number_of), total * portions[0] // sum(portions)))
    least = 1 if total - largest >= number_of - 1 else 0
    holding, spare = [largest] + [least] * (number_of - 1), total - largest - least * (number_of - 1)
    while spare > 0:
        candidates = [i for i in range(1, number_of) if holding[i] < largest] or [i for i in range(1, number_of) if holding[i] < most]
        whole, left = sum([portions[i] for i in candidates]), spare
        for i in candidates:
            extra = min(most - holding[i], max(1, left * portions[i] // whole), spare)
            holding[i] = holding[i] + extra
            spare = spare - extra
    return np.array(holding)


def gaussian(own_key, dims, deviation, reach, pieces=(), kind=jnp.bfloat16):
    values = jax.random.normal(own_key, dims, jnp.float32) * deviation
    if len(pieces) > 0:
        values = levels(own_key, dims, pieces, -0.22, 0.18) * values
    return jnp.clip(values, min=-reach, max=reach).astype(kind)


def setup_inputs(seed: int = 0) -> dict:
    seeds = jax.random.split(jax.random.key(seed), 11)
    queries = draw_queries(jax.random.fold_in(seeds[10], 71), 0)
    keys = draw_keys(jax.random.fold_in(seeds[10], 71), 0)
    values = gaussian(seeds[2], (TOKENS, KV_HEADS * HD), 4.0, 16.0, ((0, 64), (1, 8)))
    residual = draw_residual(jax.random.fold_in(seeds[10], 71), 0)
    norm_gain = jnp.clip(1.0 + 0.1 * jax.random.normal(seeds[4], (D,), jnp.float32), 0.5, 1.5)
    routes_keys = jax.random.split(jax.random.fold_in(seeds[5], 1), TOKENS // TOK_DEV)
    routes_turns = jax.random.permutation(jax.random.fold_in(seeds[5], 3), TOKENS // TOK_DEV)
    routes = jax.vmap(lambda own, number: assign_block(jax.random.fold_in(seeds[5], 2), own, number, TOK_DEV, EXPERTS, 1, CAP, 2))(routes_keys, routes_turns).reshape((TOKENS, 1))
    route_weight = jnp.clip(jnp.exp(math.log(1.0) - 1.3862944 * jax.random.uniform(seeds[6], (TOKENS,), jnp.float32) ** levels(seeds[6], (TOKENS,), ((0, 64),), -0.2, 0.2)), 0.25, 1.0)
    w_gate = gaussian(seeds[7], (EXPERTS * FF, D), D ** -0.5, 0.078125, ((0, 64), (1, 8)))
    w_up = gaussian(seeds[8], (EXPERTS * FF, D), D ** -0.5, 0.078125, ((0, 64), (1, 8)))
    w_down = gaussian(seeds[9], (EXPERTS * FF, D), FF ** -0.5, 0.046875, ((0, 64), (1, 8)))
    return {"queries": queries, "keys": keys, "values": values, "residual": residual, "norm_gain": norm_gain, "routes": routes, "route_weight": route_weight, "w_gate": w_gate, "w_up": w_up, "w_down": w_down}


def attention_heads(queries, keys, values):
    group_size = H // KV_HEADS
    score_scale = 1.0 / math.sqrt(HD)
    query_heads = queries.reshape(TOKENS, H, HD).transpose(1, 0, 2)
    key_heads = keys.reshape(TOKENS, KV_HEADS, HD).transpose(1, 0, 2)
    value_heads = values.reshape(TOKENS, KV_HEADS, HD).transpose(1, 0, 2)
    positions = jnp.arange(TOKENS, dtype=jnp.int32)
    causal = positions[None, :] <= positions[:, None]

    def one_head(head_index):
        shared = head_index // group_size
        query_rows = lax.dynamic_index_in_dim(query_heads, head_index, 0, keepdims=False)
        key_rows = lax.dynamic_index_in_dim(key_heads, shared, 0, keepdims=False)
        value_rows = lax.dynamic_index_in_dim(value_heads, shared, 0, keepdims=False)
        scores = jnp.dot(query_rows, key_rows.T, preferred_element_type=jnp.float32) * score_scale
        scores = jnp.where(causal, scores, -jnp.inf)
        row_max = lax.optimization_barrier(jnp.max(scores, axis=1, keepdims=True))
        weights = jnp.exp(scores - row_max)
        denom = lax.optimization_barrier(jnp.sum(weights, axis=1, keepdims=True))
        numer = jnp.dot(weights.astype(jnp.bfloat16), value_rows, preferred_element_type=jnp.float32)
        return numer / denom
    heads_out = lax.map(one_head, jnp.arange(H, dtype=jnp.int32))
    return heads_out.transpose(1, 0, 2).reshape(TOKENS, D).astype(jnp.bfloat16)

def reference(queries, keys, values, residual, norm_gain, routes, route_weight, w_gate, w_up, w_down):
    attn = attention_heads(queries, keys, values)
    mixed = residual.astype(jnp.float32) + attn.astype(jnp.float32)
    mean_sq = lax.optimization_barrier(jnp.mean(mixed * mixed, axis=1, keepdims=True))
    normed = (mixed * lax.rsqrt(mean_sq + 1e-05) * norm_gain[None, :]).astype(jnp.bfloat16)
    chosen = routes[:, 0].astype(jnp.int32)
    blocks = chosen.reshape(N_CTX, TOK_DEV)
    onehot = (blocks[:, :, None] == jnp.arange(EXPERTS, dtype=jnp.int32)[None, None, :]).astype(jnp.int32)
    rank = jnp.cumsum(onehot, axis=1) - 1
    slot_index = lax.optimization_barrier(jnp.sum(rank * onehot, axis=2))
    per_expert = N_CTX * CAP
    dest = (blocks * per_expert + jnp.arange(N_CTX, dtype=jnp.int32)[:, None] * CAP + slot_index).reshape(TOKENS).astype(jnp.int32)
    owner = jnp.full((EXPERTS * per_expert,), TOKENS, dtype=jnp.int32).at[dest].set(jnp.arange(TOKENS, dtype=jnp.int32))
    padded = jnp.concatenate([normed, jnp.zeros((1, D), jnp.bfloat16)], axis=0)
    token_rows = padded[owner]
    feat_block = D // N_EXP
    outputs = []
    for expert in range(EXPERTS):
        rows_here = token_rows[expert * per_expert:(expert + 1) * per_expert]
        gate_rows = w_gate[expert * FF:(expert + 1) * FF]
        up_rows = w_up[expert * FF:(expert + 1) * FF]
        down_rows = w_down[expert * FF:(expert + 1) * FF]
        gate = jnp.zeros((per_expert, FF), jnp.float32)
        up = jnp.zeros((per_expert, FF), jnp.float32)
        for block_index in range(N_EXP):
            lo = block_index * feat_block
            hi = lo + feat_block
            gate_part = jnp.dot(rows_here[:, lo:hi], gate_rows[:, lo:hi].T, preferred_element_type=jnp.float32).astype(jnp.bfloat16)
            up_part = jnp.dot(rows_here[:, lo:hi], up_rows[:, lo:hi].T, preferred_element_type=jnp.float32).astype(jnp.bfloat16)
            gate_part = lax.optimization_barrier(gate_part)
            up_part = lax.optimization_barrier(up_part)
            gate = gate + gate_part.astype(jnp.float32)
            up = up + up_part.astype(jnp.float32)
        hidden = (jax.nn.silu(gate) * up).astype(jnp.bfloat16)
        outputs.append(jnp.dot(hidden, down_rows, preferred_element_type=jnp.float32))
    expert_out = jnp.concatenate(outputs, axis=0)[dest]
    return (route_weight[:, None] * expert_out).astype(jnp.bfloat16)
```

```python
import math

import jax
import jax.numpy as jnp
from jax import lax
from jax.sharding import Mesh, PartitionSpec as P

D = 6144
HD = 128
EXPERTS = 4
CAP = 24
CHUNKS = 2
F32 = jnp.float32
BF16 = jnp.bfloat16

CTX = ("yh", "xh", "xl", "z")
EXP = ("yl", "c")
HALF = ("xh", "xl", "z")
SWAP = [(0, 1), (1, 0)]
Y_XOR = [[(i, i ^ k) for i in range(4)] for k in range(4)]


def swap(x, axis):
    return lax.ppermute(x, axis, SWAP)


def split3(v):
    hi = lax.reduce_precision(v, 8, 7)
    mid = lax.reduce_precision(v - hi, 8, 7)
    lo = (v - hi) - mid
    return [p.astype(BF16) for p in (hi, mid, lo)]


def attend(queries, keys, values):
    rows = queries.shape[0]
    heads = queries.shape[1] // HD
    yh = lax.axis_index("yh")
    scale = 1.0 / math.sqrt(HD)

    foreign = lax.ppermute(queries, "yh", [(1, 0)])
    kv = jnp.concatenate([keys, values], axis=1)
    members = lax.axis_size(HALF)
    kv = lax.all_to_all(
        jnp.broadcast_to(kv[None], (members,) + kv.shape), HALF, split_axis=0, concat_axis=0, tiled=True
    ).reshape(members * rows, 2 * HD)
    k_all, v_all = kv[:, :HD], kv[:, HD:]
    count = members * rows

    def stacked(q):
        return q.reshape(rows, heads, HD).transpose(1, 0, 2).reshape(heads * rows, HD)

    q_all = jnp.concatenate([stacked(queries), stacked(foreign)], axis=0)
    own_pos = lax.axis_index(HALF) * rows + jnp.tile(jnp.arange(rows, dtype=jnp.int32), heads)
    limit = jnp.concatenate([own_pos, jnp.full_like(own_pos, count)])
    scores = jnp.einsum("qd,kd->qk", q_all, k_all, preferred_element_type=F32) * scale
    allowed = jnp.arange(count, dtype=jnp.int32)[None, :] <= limit[:, None]
    scores = jnp.where(allowed, scores, -1e30)
    top = jnp.max(scores, axis=1)
    weights = jnp.exp(scores - top[:, None])
    total = jnp.sum(weights, axis=1)
    acc = jnp.einsum("qk,kd->qd", weights.astype(BF16), v_all, preferred_element_type=F32)
    out = acc / total[:, None]
    lse = top + jnp.log(total)

    n = heads * rows

    def unstacked(o):
        return o.reshape(heads, rows, HD).transpose(1, 0, 2).reshape(rows, heads * HD)

    out_own, out_far = unstacked(out[:n]), unstacked(out[n:])
    lse_own, lse_far = lse[:n].reshape(heads, rows).T, lse[n:].reshape(heads, rows).T
    tail = jnp.concatenate(split3(lse_far), axis=1)
    tail = jnp.pad(tail, ((0, 0), (0, HD - tail.shape[1])))
    message = jnp.concatenate([out_far.astype(BF16), tail], axis=1)
    got = lax.ppermute(message, "yh", [(0, 1)])
    got_out = got[:, : heads * HD].astype(F32)
    parts = got[:, heads * HD : heads * HD + 3 * heads].astype(F32)
    got_lse = parts[:, :heads] + parts[:, heads : 2 * heads] + parts[:, 2 * heads :]
    share = jnp.where(yh == 1, jax.nn.sigmoid(got_lse - lse_own), 0.0)
    share = jnp.repeat(share, HD, axis=1)
    return (out_own * (1.0 - share) + got_out * share).astype(BF16)


def body(queries, keys, values, residual, norm_gain, routes, route_weight, w_gate, w_up, w_down):
    rows = queries.shape[0]
    feat = residual.shape[1]
    hidden_local = w_gate.shape[0]
    half = hidden_local // 2
    core = lax.axis_index("c")

    def halves(w, which):
        return lax.dynamic_slice_in_dim(w, which * half, half, axis=0)

    w_in = jnp.concatenate([halves(w_gate, core), halves(w_up, core)], axis=0)
    w_in_other = swap(jnp.concatenate([halves(w_gate, 1 - core), halves(w_up, 1 - core)], axis=0), "c")
    w_out = halves(w_down, core)
    w_out_other = halves(w_down, 1 - core)

    attn = attend(queries, keys, values)
    mixed = residual.astype(F32) + attn.astype(F32)
    total_squares = lax.psum(jnp.sum(mixed * mixed, axis=1), EXP)
    normed = (mixed * lax.rsqrt(total_squares / D + 1e-05)[:, None] * norm_gain[None, :]).astype(BF16)

    chosen = routes[:, 0]
    expert_ids = jnp.arange(EXPERTS, dtype=jnp.int32)
    onehot = (chosen[:, None] == expert_ids[None, :]).astype(jnp.int32)
    slot_index = jnp.sum((jnp.cumsum(onehot, axis=0) - 1) * onehot, axis=1)
    slot_ids = jnp.arange(CAP, dtype=jnp.int32)
    select = (
        (chosen[None, None, :] == expert_ids[:, None, None])
        & (slot_index[None, None, :] == slot_ids[None, :, None])
    ).astype(BF16)
    packed = jnp.einsum("ect,td->ecd", select, normed, preferred_element_type=F32).astype(BF16)
    incoming = lax.all_to_all(packed, ("yh", "xh"), split_axis=0, concat_axis=0, tiled=True)

    nz = lax.axis_size("z")
    ny = lax.axis_size("yl")
    slots = CAP // CHUNKS
    block = EXPERTS * slots
    outs = []
    for k in range(CHUNKS):
        part = incoming[:, k * slots : (k + 1) * slots].reshape(block, feat)
        near = lax.all_to_all(
            jnp.broadcast_to(part[None], (nz, block, feat)), "z", split_axis=0, concat_axis=0, tiled=True
        ).reshape(nz * block, feat)
        x = jnp.concatenate([near, swap(near, "xl")], axis=0)
        x_other = swap(x, "c")
        gate_up = (
            jnp.einsum("rd,fd->rf", x, w_in, preferred_element_type=F32)
            + jnp.einsum("rd,fd->rf", x_other, w_in_other, preferred_element_type=F32)
        )
        n_rows = gate_up.shape[0]
        share = n_rows // ny
        gate_up = gate_up.astype(BF16).reshape(ny, share, 2 * half)
        me = lax.axis_index("yl")

        def piece(i):
            return lax.dynamic_index_in_dim(gate_up, me ^ i, 0, keepdims=False)

        full = piece(0).astype(F32)
        for i in range(1, ny):
            full = full + lax.ppermute(piece(i), "yl", Y_XOR[i]).astype(F32)
        hidden = (jax.nn.silu(full[:, :half]) * full[:, half:]).astype(BF16)
        hid = jnp.zeros((ny, share, half), BF16)
        hid = lax.dynamic_update_index_in_dim(hid, hidden, me, 0)
        for i in range(1, ny):
            hid = lax.dynamic_update_index_in_dim(hid, lax.ppermute(hidden, "yl", Y_XOR[i]), me ^ i, 0)
        hid = hid.reshape(n_rows, half)
        hid_other = swap(hid, "c")
        down = (
            jnp.dot(hid, w_out, preferred_element_type=F32)
            + jnp.dot(hid_other, w_out_other, preferred_element_type=F32)
        )
        stay, leave = down[: n_rows // 2], down[n_rows // 2 :]
        summed = (stay + swap(leave.astype(BF16), "xl").astype(F32)).astype(BF16)
        back = lax.all_to_all(summed.reshape(nz, block, feat), "z", split_axis=0, concat_axis=0, tiled=True)
        outs.append(jnp.sum(back.astype(F32), axis=0).astype(BF16).reshape(EXPERTS, slots, feat))
    out = jnp.concatenate(outs, axis=1)
    returned = lax.all_to_all(out, ("yh", "xh"), split_axis=0, concat_axis=0, tiled=True)
    moe_rows = jnp.einsum("ect,ecd->td", select, returned, preferred_element_type=F32)
    return (route_weight[:, None] * moe_rows).astype(BF16)


def solution(mesh):
    fine = Mesh(mesh.devices.reshape(2, 2, 2, 8, 4, 2), CTX + EXP)
    wide = P(CTX, EXP)
    in_specs = (wide, wide, wide, wide, P(EXP), P(CTX, None), P(CTX), wide, wide, wide)
    return jax.shard_map(body, mesh=fine, in_specs=in_specs, out_specs=wide, check_vma=False)
```

```python
import math
from functools import partial

import jax
import jax.numpy as jnp
from jax import lax
from jax.experimental import pallas as pl
from jax.experimental.pallas import tpu as pltpu
from jax.sharding import Mesh, PartitionSpec as P

D = 6144
HD = 128
EXPERTS = 4
CAP = 24
SLOTS = (8, 8, 8)
F32 = jnp.float32
BF16 = jnp.bfloat16

CTX = ("yh", "xh", "xl", "z")
EXP = ("yl", "c")
HALF = ("xh", "xl", "z")
ROUTE = ("yh", "xh", "z")
SWAP = [(0, 1), (1, 0)]
Y_XOR = [[(i, i ^ k) for i in range(4)] for k in range(4)]
RELATIVE = (0, 2, 1, 3)


def swap(x, axis):
    return lax.ppermute(x, axis, SWAP)


def split3(v):
    hi = lax.reduce_precision(v, 8, 7)
    mid = lax.reduce_precision(v - hi, 8, 7)
    lo = (v - hi) - mid
    return [p.astype(BF16) for p in (hi, mid, lo)]


def attend(queries, keys, values, early, late):
    rows = queries.shape[0]
    heads = queries.shape[1] // HD
    yh = lax.axis_index("yh")
    scale = 1.0 / math.sqrt(HD)

    foreign = lax.ppermute(queries, "yh", [(1, 0)])
    kv = jnp.concatenate([keys, values], axis=1)
    members = lax.axis_size(HALF)
    kv = lax.all_to_all(
        jnp.broadcast_to(kv[None], (members,) + kv.shape), HALF, split_axis=0, concat_axis=0, tiled=True
    ).reshape(members * rows, 2 * HD)
    kv, *early = lax.optimization_barrier((kv,) + early)
    k_all, v_all = kv[:, :HD], kv[:, HD:]
    count = members * rows

    def stacked(q):
        return q.reshape(rows, heads, HD).transpose(1, 0, 2).reshape(heads * rows, HD)

    q_all = jnp.concatenate([stacked(queries), stacked(foreign)], axis=0)
    own_pos = lax.axis_index(HALF) * rows + jnp.tile(jnp.arange(rows, dtype=jnp.int32), heads)
    limit = jnp.concatenate([own_pos, jnp.full_like(own_pos, count)])
    scores = jnp.einsum("qd,kd->qk", q_all, k_all, preferred_element_type=F32) * scale
    allowed = jnp.arange(count, dtype=jnp.int32)[None, :] <= limit[:, None]
    scores = jnp.where(allowed, scores, -1e30)
    top = jnp.max(scores, axis=1)
    weights = jnp.exp(scores - top[:, None])
    total = jnp.sum(weights, axis=1)
    acc = jnp.einsum("qk,kd->qd", weights.astype(BF16), v_all, preferred_element_type=F32)
    out = acc / total[:, None]
    lse = top + jnp.log(total)

    n = heads * rows

    def unstacked(o):
        return o.reshape(heads, rows, HD).transpose(1, 0, 2).reshape(rows, heads * HD)

    out_own, out_far = unstacked(out[:n]), unstacked(out[n:])
    lse_own, lse_far = lse[:n].reshape(heads, rows).T, lse[n:].reshape(heads, rows).T
    tail = jnp.concatenate(split3(lse_far), axis=1)
    tail = jnp.pad(tail, ((0, 0), (0, HD - tail.shape[1])))
    message = jnp.concatenate([out_far.astype(BF16), tail], axis=1)
    message, *late = lax.optimization_barrier((message,) + late)
    got = lax.ppermute(message, "yh", [(0, 1)])
    got_out = got[:, : heads * HD].astype(F32)
    parts = got[:, heads * HD : heads * HD + 3 * heads].astype(F32)
    got_lse = parts[:, :heads] + parts[:, heads : 2 * heads] + parts[:, 2 * heads :]
    share = jnp.where(yh == 1, jax.nn.sigmoid(got_lse - lse_own), 0.0)
    share = jnp.repeat(share, HD, axis=1)
    return (out_own * (1.0 - share) + got_out * share).astype(BF16), early, late


def expand(order_ref, x_ref, xo_ref, wn_ref, won_ref, wf_ref, wof_ref, keep_ref, send_ref, acc_ref):
    step = pl.program_id(0)
    contract = (((1,), (1,)), ((), ()))

    def terms(a, b):
        return lax.dot_general(x_ref[...], a[...], contract, preferred_element_type=F32) + lax.dot_general(
            xo_ref[...], b[...], contract, preferred_element_type=F32
        )

    @pl.when(step < 2)
    def _():
        acc_ref[...] = terms(wn_ref, won_ref)

    @pl.when(step >= 2)
    def _():
        acc_ref[...] = terms(wf_ref, wof_ref)

    share = keep_ref.shape[1]
    for p in range(2):
        for ref, i in ((keep_ref, 2 * p), (send_ref, 2 * p + 1)):
            at = pl.multiple_of((order_ref[0] ^ i) * share, share)
            ref[p] = acc_ref[pl.ds(at, share), :].astype(BF16)


def gate_up_terms(order, x, xo, w, wo, wf, wof):
    rows, feat = x.shape
    cols = w.shape[0] // 2
    share = rows // 4
    full = pl.BlockSpec((rows, feat), lambda n, o: (0, 0))
    near = pl.BlockSpec((cols, feat), lambda n, o: (jnp.minimum(n, 1), 0))
    far = pl.BlockSpec((cols, feat), lambda n, o: (jnp.maximum(n - 2, 0), 0))
    out = pl.BlockSpec((2, share, cols), lambda n, o: (0, 0, n))
    shape = jax.ShapeDtypeStruct((2, share, 4 * cols), BF16)
    return pl.pallas_call(
        expand,
        grid_spec=pltpu.PrefetchScalarGridSpec(
            num_scalar_prefetch=1,
            grid=(4,),
            in_specs=[full, full, near, near, far, far],
            out_specs=[out, out],
            scratch_shapes=[pltpu.VMEM((rows, cols), F32)],
        ),
        out_shape=[shape, shape],
        cost_estimate=pl.CostEstimate(
            flops=16 * rows * cols * feat, transcendentals=0, bytes_accessed=16 * cols * feat + 20 * rows * cols
        ),
        compiler_params=pltpu.CompilerParams(vmem_limit_bytes=40 << 20),
        name="gate_up_terms",
    )(order, x, xo, w, wo, wf, wof)


def contract_hidden(order_ref, h_ref, ho_ref, w_ref, wf_ref, out_ref):
    core = order_ref[1]
    half = w_ref.shape[0] // 2
    own = pl.multiple_of(core * half, half)
    other = pl.multiple_of((1 - core) * half, half)
    acc = jnp.dot(h_ref[:, :half], w_ref[pl.ds(own, half), :], preferred_element_type=F32)
    acc += jnp.dot(ho_ref[:, :half], w_ref[pl.ds(other, half), :], preferred_element_type=F32)
    acc += jnp.dot(h_ref[:, half:], wf_ref[pl.ds(own, half), :], preferred_element_type=F32)
    acc += jnp.dot(ho_ref[:, half:], wf_ref[pl.ds(other, half), :], preferred_element_type=F32)
    share = out_ref.shape[0] // 4
    for p, i in enumerate(RELATIVE):
        at = pl.multiple_of((order_ref[0] ^ i) * share, share)
        out_ref[pl.ds(at, share), :] = acc[p * share : (p + 1) * share].astype(BF16)


def down_terms(order, h, ho, w, wf):
    rows = h.shape[0]
    hidden, feat = w.shape
    whole = pl.BlockSpec(memory_space=pltpu.VMEM)
    return pl.pallas_call(
        contract_hidden,
        in_specs=[pl.BlockSpec(memory_space=pltpu.SMEM), whole, whole, whole, whole],
        out_specs=whole,
        out_shape=jax.ShapeDtypeStruct((rows, feat), BF16),
        cost_estimate=pl.CostEstimate(
            flops=4 * rows * hidden * feat, transcendentals=0, bytes_accessed=4 * hidden * feat + 6 * rows * hidden
        ),
        compiler_params=pltpu.CompilerParams(vmem_limit_bytes=40 << 20),
        name="down_terms",
    )(order, h, ho, w, wf)


def after(value, *others):
    return lax.optimization_barrier((value,) + others)[0]


def body(queries, keys, values, residual, norm_gain, routes, route_weight, w_gate, w_up, w_down):
    feat = residual.shape[1]
    half = w_gate.shape[0] // 2
    core = lax.axis_index("c")
    me = lax.axis_index("yl")
    order = jnp.stack([me, core]).astype(jnp.int32)

    def halves(which):
        cut = partial(lax.dynamic_slice_in_dim, start_index=which * half, slice_size=half, axis=0)
        return jnp.concatenate([cut(w_gate), cut(w_up)], axis=0)

    w_in, w_give = halves(core), halves(1 - core)
    w_in_other = swap(w_give, "c")
    w_in_far = swap(w_in, "xl")
    w_in_other_far = lax.ppermute(w_give, ("xl", "c"), [(i, 3 - i) for i in range(4)])
    w_out_far = swap(w_down, "xl")

    attn, (w_in_other, w_in_far), (w_in_other_far,) = attend(
        queries, keys, values, (w_in_other, w_in_far), (w_in_other_far,)
    )
    mixed = residual.astype(F32) + attn.astype(F32)
    total_squares = lax.psum(jnp.sum(mixed * mixed, axis=1), EXP)
    total_squares, w_out_far = lax.optimization_barrier((total_squares, w_out_far))
    normed = (mixed * lax.rsqrt(total_squares / D + 1e-05)[:, None] * norm_gain[None, :]).astype(BF16)

    chosen = routes[:, 0]
    expert_ids = jnp.arange(EXPERTS, dtype=jnp.int32)
    onehot = (chosen[:, None] == expert_ids[None, :]).astype(jnp.int32)
    slot_index = jnp.sum((jnp.cumsum(onehot, axis=0) - 1) * onehot, axis=1)
    slot_ids = jnp.arange(CAP, dtype=jnp.int32)
    select = (
        (chosen[None, None, :] == expert_ids[:, None, None])
        & (slot_index[None, None, :] == slot_ids[None, :, None])
    ).astype(BF16)
    packed = jnp.einsum("ect,td->ecd", select, normed, preferred_element_type=F32).astype(BF16)

    nz = lax.axis_size("z")
    peers = EXPERTS * nz

    def dispatch(lo, n):
        part = packed[:, lo : lo + n]
        part = jnp.broadcast_to(part[:, None], (EXPERTS, nz, n, feat)).reshape(peers, n, feat)
        x = lax.all_to_all(part, ROUTE, split_axis=0, concat_axis=0, tiled=True)
        return x.reshape(peers * n, feat)

    def hidden_of(keep, send):
        got = lax.ppermute(send, "yl", Y_XOR[1])
        pair = (keep[1].astype(F32) + got[1].astype(F32)).astype(BF16)
        last = lax.ppermute(pair, "yl", Y_XOR[2])
        full = keep[0].astype(F32) + got[0].astype(F32) + last.astype(F32)
        near = jax.nn.silu(full[:, :half]) * full[:, half : 2 * half]
        far = jax.nn.silu(full[:, 2 * half : 3 * half]) * full[:, 3 * half :]
        return jnp.concatenate([near, far], axis=1).astype(BF16)

    def spread(hidden):
        two = jnp.concatenate([hidden, lax.ppermute(hidden, "yl", Y_XOR[2])], axis=0)
        return jnp.concatenate([two, lax.ppermute(two, "yl", Y_XOR[1])], axis=0)

    def give_back(down, n):
        back = lax.all_to_all(down.reshape(peers, n, feat), ROUTE, split_axis=0, concat_axis=0, tiled=True)
        return jnp.sum(back.reshape(EXPERTS, nz, n, feat).astype(F32), axis=1).astype(BF16)

    starts = [sum(SLOTS[:k]) for k in range(len(SLOTS))]
    terms = []
    for lo, n in zip(starts, SLOTS):
        x = dispatch(lo, n)
        if terms:
            x = after(x, *terms[-1])
        terms.append(gate_up_terms(order, x, swap(x, "c"), w_in, w_in_other, w_in_far, w_in_other_far))
    outs = []
    for (keep, send), n in zip(terms, SLOTS):
        hid = spread(hidden_of(keep, send))
        outs.append(give_back(down_terms(order, hid, swap(hid, "c"), w_down, w_out_far), n))
    returned = jnp.concatenate(outs, axis=1)
    moe_rows = jnp.einsum("ect,ecd->td", select, returned, preferred_element_type=F32)
    return (route_weight[:, None] * moe_rows).astype(BF16)


def solution(mesh):
    fine = Mesh(mesh.devices.reshape(2, 2, 2, 8, 4, 2), CTX + EXP)
    wide = P(CTX, EXP)
    in_specs = (wide, wide, wide, wide, P(EXP), P(CTX, None), P(CTX), wide, wide, wide)
    return jax.shard_map(body, mesh=fine, in_specs=in_specs, out_specs=wide, check_vma=False)
```

```python
import math
from functools import partial

import jax
import jax.numpy as jnp
from jax import lax
from jax.experimental import pallas as pl
from jax.experimental.pallas import tpu as pltpu
from jax.sharding import Mesh, PartitionSpec as P

D = 6144
HD = 128
EXPERTS = 4
CAP = 24
SLOT = 8
F32 = jnp.float32
BF16 = jnp.bfloat16

CTX = ("yh", "xh", "xl", "z")
EXP = ("yl", "c")
HALF = ("xh", "xl", "z")
GROUP = ("yh", "xh")
SWAP = [(0, 1), (1, 0)]
Y_XOR = [[(i, i ^ k) for i in range(4)] for k in range(4)]


def swap(x, axis):
    return lax.ppermute(x, axis, SWAP)


def split3(v):
    hi = lax.reduce_precision(v, 8, 7)
    mid = lax.reduce_precision(v - hi, 8, 7)
    lo = (v - hi) - mid
    return [p.astype(BF16) for p in (hi, mid, lo)]


def attend(queries, keys, values, early):
    rows = queries.shape[0]
    heads = queries.shape[1] // HD
    yh = lax.axis_index("yh")
    scale = 1.0 / math.sqrt(HD)

    foreign = lax.ppermute(queries, "yh", [(1, 0)])
    kv = jnp.concatenate([keys, values], axis=1)
    members = lax.axis_size(HALF)
    kv = lax.all_to_all(
        jnp.broadcast_to(kv[None], (members,) + kv.shape), HALF, split_axis=0, concat_axis=0, tiled=True
    ).reshape(members * rows, 2 * HD)
    kv, *early = lax.optimization_barrier((kv,) + early)
    k_all, v_all = kv[:, :HD], kv[:, HD:]
    count = members * rows

    def stacked(q):
        return q.reshape(rows, heads, HD).transpose(1, 0, 2).reshape(heads * rows, HD)

    q_all = jnp.concatenate([stacked(queries), stacked(foreign)], axis=0)
    own_pos = lax.axis_index(HALF) * rows + jnp.tile(jnp.arange(rows, dtype=jnp.int32), heads)
    limit = jnp.concatenate([own_pos, jnp.full_like(own_pos, count)])
    scores = jnp.einsum("qd,kd->qk", q_all, k_all, preferred_element_type=F32) * scale
    allowed = jnp.arange(count, dtype=jnp.int32)[None, :] <= limit[:, None]
    scores = jnp.where(allowed, scores, -1e30)
    top = jnp.max(scores, axis=1)
    weights = jnp.exp(scores - top[:, None])
    total = jnp.sum(weights, axis=1)
    acc = jnp.einsum("qk,kd->qd", weights.astype(BF16), v_all, preferred_element_type=F32)
    out = acc / total[:, None]
    lse = top + jnp.log(total)

    n = heads * rows

    def unstacked(o):
        return o.reshape(heads, rows, HD).transpose(1, 0, 2).reshape(rows, heads * HD)

    out_own, out_far = unstacked(out[:n]), unstacked(out[n:])
    lse_own, lse_far = lse[:n].reshape(heads, rows).T, lse[n:].reshape(heads, rows).T
    tail = jnp.concatenate(split3(lse_far), axis=1)
    tail = jnp.pad(tail, ((0, 0), (0, HD - tail.shape[1])))
    message = jnp.concatenate([out_far.astype(BF16), tail], axis=1)
    got = lax.ppermute(message, "yh", [(0, 1)])
    got_out = got[:, : heads * HD].astype(F32)
    parts = got[:, heads * HD : heads * HD + 3 * heads].astype(F32)
    got_lse = parts[:, :heads] + parts[:, heads : 2 * heads] + parts[:, 2 * heads :]
    share = jnp.where(yh == 1, jax.nn.sigmoid(got_lse - lse_own), 0.0)
    share = jnp.repeat(share, HD, axis=1)
    return (out_own * (1.0 - share) + got_out * share).astype(BF16), early


def expand(order_ref, xn_ref, xf_ref, on_ref, of_ref, w_ref, wo_ref, *rest):
    out_refs, acc_ref = rest[:4], rest[4]
    contract = (((1,), (1,)), ((), ()))
    rows = acc_ref.shape[0] // 2
    for p, (a, b) in enumerate(((xn_ref, on_ref), (xf_ref, of_ref))):
        a, b = (r[...].reshape(rows, r.shape[-1]) for r in (a, b))
        acc_ref[p * rows : (p + 1) * rows, :] = lax.dot_general(
            a, w_ref[...], contract, preferred_element_type=F32
        ) + lax.dot_general(b, wo_ref[...], contract, preferred_element_type=F32)
    share = out_refs[0].shape[0]
    for i, ref in enumerate(out_refs):
        at = pl.multiple_of((order_ref[0] ^ i) * share, share)
        ref[...] = acc_ref[pl.ds(at, share), :].astype(BF16)


def gate_up_terms(order, near, far, near_other, far_other, specs, w, wo, rows):
    hidden, feat = w.shape
    cols = hidden // 2
    share = rows // 4
    weight = pl.BlockSpec((cols, feat), lambda n, o: (n, 0))
    out = pl.BlockSpec((share, cols), lambda n, o: (0, n))
    shape = jax.ShapeDtypeStruct((share, hidden), BF16)
    return pl.pallas_call(
        expand,
        grid_spec=pltpu.PrefetchScalarGridSpec(
            num_scalar_prefetch=1,
            grid=(2,),
            in_specs=[specs[0], specs[1], specs[0], specs[1], weight, weight],
            out_specs=[out] * 4,
            scratch_shapes=[pltpu.VMEM((rows, cols), F32)],
        ),
        out_shape=[shape] * 4,
        cost_estimate=pl.CostEstimate(
            flops=4 * rows * hidden * feat, transcendentals=0, bytes_accessed=4 * hidden * feat + 2 * rows * hidden
        ),
        compiler_params=pltpu.CompilerParams(vmem_limit_bytes=40 << 20),
        name="gate_up_terms",
    )(order, near, far, near_other, far_other, w, wo)


def contract_hidden(order_ref, h_ref, ho_ref, w_ref, near_ref, far_ref):
    core = order_ref[1]
    half = w_ref.shape[0] // 2
    own = pl.multiple_of(core * half, half)
    other = pl.multiple_of((1 - core) * half, half)
    acc = jnp.dot(h_ref[...], w_ref[pl.ds(own, half), :], preferred_element_type=F32)
    acc += jnp.dot(ho_ref[...], w_ref[pl.ds(other, half), :], preferred_element_type=F32)
    share = h_ref.shape[0] // 4
    for i in range(4):
        block = order_ref[0] ^ i
        at = pl.multiple_of((block & 1) * share, share)
        part = acc[i * share : (i + 1) * share].astype(BF16)

        @pl.when(block < 2)
        def _():
            near_ref[pl.ds(at, share), :] = part

        @pl.when(block >= 2)
        def _():
            far_ref[pl.ds(at, share), :] = part


def down_terms(order, h, ho, w):
    rows = h.shape[0]
    hidden, feat = w.shape
    whole = pl.BlockSpec(memory_space=pltpu.VMEM)
    shape = jax.ShapeDtypeStruct((rows // 2, feat), BF16)
    return pl.pallas_call(
        contract_hidden,
        in_specs=[pl.BlockSpec(memory_space=pltpu.SMEM), whole, whole, whole],
        out_specs=[whole, whole],
        out_shape=[shape, shape],
        cost_estimate=pl.CostEstimate(
            flops=2 * rows * hidden * feat, transcendentals=0, bytes_accessed=2 * hidden * feat + 4 * rows * hidden
        ),
        compiler_params=pltpu.CompilerParams(vmem_limit_bytes=40 << 20),
        name="down_terms",
    )(order, h, ho, w)


def after(value, *others):
    return lax.optimization_barrier((value,) + others)[0]


def exchange(blocks, axes):
    me = lax.axis_index(axes)
    xor = [[(i, i ^ k) for i in range(4)] for k in range(4)]
    got = jnp.zeros_like(blocks)
    for k in range(4):
        block = lax.dynamic_index_in_dim(blocks, me ^ k, 0, keepdims=False)
        if k:
            block = lax.ppermute(block, axes, xor[k])
        got = lax.dynamic_update_index_in_dim(got, block, me ^ k, 0)
    return got


def body(queries, keys, values, residual, norm_gain, routes, route_weight, w_gate, w_up, w_down):
    feat = residual.shape[1]
    half = w_gate.shape[0] // 2
    core = lax.axis_index("c")
    me = lax.axis_index("yl")
    xl = lax.axis_index("xl")
    order = jnp.stack([me, core, xl]).astype(jnp.int32)

    def halves(which):
        cut = partial(lax.dynamic_slice_in_dim, start_index=which * half, slice_size=half, axis=0)
        return jnp.concatenate([cut(w_gate), cut(w_up)], axis=0)

    w_in = halves(core)
    w_in_other = swap(halves(1 - core), "c")

    attn, (w_in, w_in_other) = attend(queries, keys, values, (w_in, w_in_other))
    mixed = residual.astype(F32) + attn.astype(F32)
    total_squares = lax.psum(jnp.sum(mixed * mixed, axis=1), EXP)
    normed = (mixed * lax.rsqrt(total_squares / D + 1e-05)[:, None] * norm_gain[None, :]).astype(BF16)

    chosen = routes[:, 0]
    expert_ids = jnp.arange(EXPERTS, dtype=jnp.int32)
    onehot = (chosen[:, None] == expert_ids[None, :]).astype(jnp.int32)
    slot_index = jnp.sum((jnp.cumsum(onehot, axis=0) - 1) * onehot, axis=1)
    slot_ids = jnp.arange(CAP, dtype=jnp.int32)
    select = (
        (chosen[None, None, :] == expert_ids[:, None, None])
        & (slot_index[None, None, :] == slot_ids[None, :, None])
    ).astype(BF16)
    packed = jnp.einsum("ect,td->ecd", select, normed, preferred_element_type=F32).astype(BF16)

    nx = lax.axis_size("xl")
    nz = lax.axis_size("z")
    n = SLOT
    group = EXPERTS * n
    rows = nx * nz * group

    direct = jnp.broadcast_to(packed[:, None, :n], (EXPERTS, nx * nz, n, feat)).reshape(-1, n, feat)
    x_a = lax.all_to_all(direct, CTX, split_axis=0, concat_axis=0, tiled=True).reshape(EXPERTS, nx, nz * n, feat)
    rest = exchange(packed[:, n:], GROUP).reshape(EXPERTS, 2, n, feat).transpose(1, 0, 2, 3).reshape(2 * group, feat)
    rest = after(rest, x_a)
    near = lax.all_to_all(
        jnp.broadcast_to(rest[None], (nz, 2 * group, feat)), "z", split_axis=0, concat_axis=0, tiled=True
    ).reshape(nz, 2, group, feat)
    x_a_other = swap(x_a, "c")
    a_block = (EXPERTS, pl.Squeezed(), nz * n, feat)
    specs_a = (
        pl.BlockSpec(a_block, lambda k, o: (0, o[2], 0, 0)),
        pl.BlockSpec(a_block, lambda k, o: (0, 1 - o[2], 0, 0)),
    )
    terms = [gate_up_terms(order, x_a, x_a, x_a_other, x_a_other, specs_a, w_in, w_in_other, rows)]
    near = after(near, *terms[0])
    far = swap(near, "xl")
    near_other, far_other = swap(near, "c"), swap(far, "c")
    for chunk in range(2):
        spec = pl.BlockSpec((nz, pl.Squeezed(), group, feat), lambda k, o, chunk=chunk: (0, chunk, 0, 0))
        first = after(far_other, *terms[-1])
        terms.append(gate_up_terms(order, near, far, near_other, first, (spec, spec), w_in, w_in_other, rows))

    def hidden_of(parts):
        full = parts[0].astype(F32)
        for i in range(1, 4):
            full = full + lax.ppermute(parts[i], "yl", Y_XOR[i]).astype(F32)
        return (jax.nn.silu(full[:, :half]) * full[:, half:]).astype(BF16)

    def down_of(parts):
        hidden = hidden_of(parts)
        hid = jnp.concatenate([hidden] + [lax.ppermute(hidden, "yl", Y_XOR[i]) for i in range(1, 4)], axis=0)
        return down_terms(order, hid, swap(hid, "c"), w_down)

    def gather_z(down, dims):
        stay, leave = down
        summed = (stay.astype(F32) + swap(leave, "xl").astype(F32)).astype(BF16)
        if dims == "ez":
            summed = summed.reshape(EXPERTS, nz, group // EXPERTS, feat).transpose(1, 0, 2, 3)
        back = lax.all_to_all(summed.reshape(nz, group, feat), "z", split_axis=0, concat_axis=0, tiled=True)
        return jnp.sum(back.astype(F32), axis=0).astype(BF16).reshape(EXPERTS, n, feat)

    out_a = gather_z(down_of(terms[0]), "ez")
    out_b = gather_z(down_of(terms[1]), "ze")
    stay, leave = (d.reshape(nz, EXPERTS, n, feat).transpose(1, 0, 2, 3) for d in down_of(terms[2]))
    direct = jnp.where(xl == 0, jnp.stack([stay, leave], axis=1), jnp.stack([leave, stay], axis=1))
    out_c = lax.all_to_all(direct.reshape(-1, n, feat), CTX, split_axis=0, concat_axis=0, tiled=True)
    out_c = jnp.sum(out_c.reshape(EXPERTS, nx * nz, n, feat).astype(F32), axis=1).astype(BF16)
    out_ab = exchange(jnp.concatenate([out_a, out_b], axis=1), GROUP)
    returned = jnp.concatenate([out_ab, out_c], axis=1)
    moe_rows = jnp.einsum("ect,ecd->td", select, returned, preferred_element_type=F32)
    return (route_weight[:, None] * moe_rows).astype(BF16)


def solution(mesh):
    fine = Mesh(mesh.devices.reshape(2, 2, 2, 8, 4, 2), CTX + EXP)
    wide = P(CTX, EXP)
    in_specs = (wide, wide, wide, wide, P(EXP), P(CTX, None), P(CTX), wide, wide, wide)
    return jax.shard_map(body, mesh=fine, in_specs=in_specs, out_specs=wide, check_vma=False)
```

```python
import math
from functools import partial

import jax
import jax.numpy as jnp
from jax import lax
from jax.experimental import pallas as pl
from jax.experimental.pallas import tpu as pltpu
from jax.sharding import Mesh, PartitionSpec as P

D = 6144
HD = 128
EXPERTS = 4
CAP = 24
F32 = jnp.float32
BF16 = jnp.bfloat16

CTX = ("yh", "xh", "xl", "z")
EXP = ("yl", "c")
HALF = ("xh", "xl", "z")
GROUP = ("yh", "xh")
ROUTE = ("yh", "xh", "z")
SWAP = [(0, 1), (1, 0)]
Y_XOR = [[(i, i ^ k) for i in range(4)] for k in range(4)]


def swap(x, axis):
    return lax.ppermute(x, axis, SWAP)


def split3(v):
    hi = lax.reduce_precision(v, 8, 7)
    mid = lax.reduce_precision(v - hi, 8, 7)
    lo = (v - hi) - mid
    return [p.astype(BF16) for p in (hi, mid, lo)]


def attend(queries, keys, values, early):
    rows = queries.shape[0]
    heads = queries.shape[1] // HD
    yh = lax.axis_index("yh")
    scale = 1.0 / math.sqrt(HD)

    foreign = lax.ppermute(queries, "yh", [(1, 0)])
    kv = jnp.concatenate([keys, values], axis=1)
    members = lax.axis_size(HALF)
    kv = lax.all_to_all(
        jnp.broadcast_to(kv[None], (members,) + kv.shape), HALF, split_axis=0, concat_axis=0, tiled=True
    ).reshape(members * rows, 2 * HD)
    kv, *early = lax.optimization_barrier((kv,) + early)
    k_all, v_all = kv[:, :HD], kv[:, HD:]
    count = members * rows

    def stacked(q):
        return q.reshape(rows, heads, HD).transpose(1, 0, 2).reshape(heads * rows, HD)

    q_all = jnp.concatenate([stacked(queries), stacked(foreign)], axis=0)
    own_pos = lax.axis_index(HALF) * rows + jnp.tile(jnp.arange(rows, dtype=jnp.int32), heads)
    limit = jnp.concatenate([own_pos, jnp.full_like(own_pos, count)])
    scores = jnp.einsum("qd,kd->qk", q_all, k_all, preferred_element_type=F32) * scale
    allowed = jnp.arange(count, dtype=jnp.int32)[None, :] <= limit[:, None]
    scores = jnp.where(allowed, scores, -1e30)
    top = jnp.max(scores, axis=1)
    weights = jnp.exp(scores - top[:, None])
    total = jnp.sum(weights, axis=1)
    acc = jnp.einsum("qk,kd->qd", weights.astype(BF16), v_all, preferred_element_type=F32)
    out = acc / total[:, None]
    lse = top + jnp.log(total)

    n = heads * rows

    def unstacked(o):
        return o.reshape(heads, rows, HD).transpose(1, 0, 2).reshape(rows, heads * HD)

    out_own, out_far = unstacked(out[:n]), unstacked(out[n:])
    lse_own, lse_far = lse[:n].reshape(heads, rows).T, lse[n:].reshape(heads, rows).T
    tail = jnp.concatenate(split3(lse_far), axis=1)
    tail = jnp.pad(tail, ((0, 0), (0, HD - tail.shape[1])))
    message = jnp.concatenate([out_far.astype(BF16), tail], axis=1)
    got = lax.ppermute(message, "yh", [(0, 1)])
    got_out = got[:, : heads * HD].astype(F32)
    parts = got[:, heads * HD : heads * HD + 3 * heads].astype(F32)
    got_lse = parts[:, :heads] + parts[:, heads : 2 * heads] + parts[:, 2 * heads :]
    share = jnp.where(yh == 1, jax.nn.sigmoid(got_lse - lse_own), 0.0)
    share = jnp.repeat(share, HD, axis=1)
    return (out_own * (1.0 - share) + got_out * share).astype(BF16), early


def expand(order_ref, xn_ref, xf_ref, on_ref, of_ref, w_ref, wo_ref, *rest):
    out_refs, acc_ref = rest[:4], rest[4]
    contract = (((1,), (1,)), ((), ()))
    rows = acc_ref.shape[0] // 2
    for p, (a, b) in enumerate(((xn_ref, on_ref), (xf_ref, of_ref))):
        a, b = (r[...].reshape(rows, r.shape[-1]) for r in (a, b))
        acc_ref[p * rows : (p + 1) * rows, :] = lax.dot_general(
            a, w_ref[...], contract, preferred_element_type=F32
        ) + lax.dot_general(b, wo_ref[...], contract, preferred_element_type=F32)
    share = out_refs[0].shape[0]
    for i, ref in enumerate(out_refs):
        at = pl.multiple_of((order_ref[0] ^ i) * share, share)
        ref[...] = acc_ref[pl.ds(at, share), :].astype(BF16)


def gate_up_terms(order, near, far, near_other, far_other, w, wo, block, chunk):
    hidden, feat = w.shape
    cols = hidden // 2
    rows = 2 * near.shape[0] * block
    share = rows // 4
    x = pl.BlockSpec((near.shape[0], block, feat), lambda n, o: (0, chunk, 0))
    weight = pl.BlockSpec((cols, feat), lambda n, o: (n, 0))
    out = pl.BlockSpec((share, cols), lambda n, o: (0, n))
    shape = jax.ShapeDtypeStruct((share, hidden), BF16)
    return pl.pallas_call(
        expand,
        grid_spec=pltpu.PrefetchScalarGridSpec(
            num_scalar_prefetch=1,
            grid=(2,),
            in_specs=[x, x, x, x, weight, weight],
            out_specs=[out] * 4,
            scratch_shapes=[pltpu.VMEM((rows, cols), F32)],
        ),
        out_shape=[shape] * 4,
        cost_estimate=pl.CostEstimate(
            flops=4 * rows * hidden * feat, transcendentals=0, bytes_accessed=4 * hidden * feat + 2 * rows * hidden
        ),
        compiler_params=pltpu.CompilerParams(vmem_limit_bytes=40 << 20),
        name="gate_up_terms",
    )(order, near, far, near_other, far_other, w, wo)


def contract_hidden(order_ref, h_ref, ho_ref, w_ref, near_ref, far_ref):
    core = order_ref[1]
    half = w_ref.shape[0] // 2
    own = pl.multiple_of(core * half, half)
    other = pl.multiple_of((1 - core) * half, half)
    acc = jnp.dot(h_ref[...], w_ref[pl.ds(own, half), :], preferred_element_type=F32)
    acc += jnp.dot(ho_ref[...], w_ref[pl.ds(other, half), :], preferred_element_type=F32)
    share = h_ref.shape[0] // 4
    for i in range(4):
        block = order_ref[0] ^ i
        at = pl.multiple_of((block & 1) * share, share)
        part = acc[i * share : (i + 1) * share].astype(BF16)

        @pl.when(block < 2)
        def _():
            near_ref[pl.ds(at, share), :] = part

        @pl.when(block >= 2)
        def _():
            far_ref[pl.ds(at, share), :] = part


def down_terms(order, h, ho, w):
    rows = h.shape[0]
    hidden, feat = w.shape
    whole = pl.BlockSpec(memory_space=pltpu.VMEM)
    shape = jax.ShapeDtypeStruct((rows // 2, feat), BF16)
    return pl.pallas_call(
        contract_hidden,
        in_specs=[pl.BlockSpec(memory_space=pltpu.SMEM), whole, whole, whole],
        out_specs=[whole, whole],
        out_shape=[shape, shape],
        cost_estimate=pl.CostEstimate(
            flops=2 * rows * hidden * feat, transcendentals=0, bytes_accessed=2 * hidden * feat + 4 * rows * hidden
        ),
        compiler_params=pltpu.CompilerParams(vmem_limit_bytes=40 << 20),
        name="down_terms",
    )(order, h, ho, w)


def after(value, *others):
    return lax.optimization_barrier((value,) + others)[0]


def as_rows(v, feat):
    row = jnp.concatenate(split3(v), axis=-1)
    return jnp.pad(row[..., None, :], [(0, 0)] * (v.ndim - 1) + [(0, 7), (0, feat - row.shape[-1])])


def from_row(row, n):
    hi, mid, lo = (row[..., k * n : (k + 1) * n].astype(F32) for k in range(3))
    return hi + mid + lo


def body(queries, keys, values, residual, norm_gain, routes, route_weight, w_gate, w_up, w_down):
    feat = residual.shape[1]
    half = w_gate.shape[0] // 2
    core = lax.axis_index("c")
    me = lax.axis_index("yl")
    order = jnp.stack([me, core]).astype(jnp.int32)

    def halves(which):
        cut = partial(lax.dynamic_slice_in_dim, start_index=which * half, slice_size=half, axis=0)
        return jnp.concatenate([cut(w_gate), cut(w_up)], axis=0)

    w_in = halves(core)
    w_in_other = swap(halves(1 - core), "c")

    chosen = routes[:, 0]
    expert_ids = jnp.arange(EXPERTS, dtype=jnp.int32)
    onehot = (chosen[:, None] == expert_ids[None, :]).astype(jnp.int32)
    slot_index = jnp.sum((jnp.cumsum(onehot, axis=0) - 1) * onehot, axis=1)
    slot_ids = jnp.arange(CAP, dtype=jnp.int32)
    taken = (chosen[None, None, :] == expert_ids[:, None, None]) & (
        slot_index[None, None, :] == slot_ids[None, :, None]
    )
    select = taken.astype(BF16)

    attn, (w_in, w_in_other) = attend(queries, keys, values, (w_in, w_in_other))
    mixed = residual.astype(F32) + attn.astype(F32)
    squares = jnp.sum(mixed * mixed, axis=1)
    packed = jnp.einsum(
        "ect,td->ecd", select, (mixed * norm_gain[None, :]).astype(BF16), preferred_element_type=F32
    ).astype(BF16)

    nz = lax.axis_size("z")
    n = CAP // 3
    group = EXPERTS * n
    rows = nz * group

    def all_to_all(x, axes):
        return lax.all_to_all(x, axes, split_axis=0, concat_axis=0, tiled=True)

    x_a = jnp.broadcast_to(packed[:, None, :n], (EXPERTS, nz, n, feat)).reshape(-1, n, feat)
    x_a = all_to_all(x_a, ROUTE)
    inverse = lax.rsqrt(lax.psum(squares, EXP) / D + 1e-05)
    inverse = jnp.sum(jnp.where(taken, inverse[None, None, :], 0.0), axis=2)
    x_a, inverse = lax.optimization_barrier((x_a, inverse))
    x_a = x_a.reshape(EXPERTS, nz * n, feat)
    far_a = swap(x_a, "xl")
    rest = all_to_all(jnp.concatenate([packed[:, n:], as_rows(inverse, feat)], axis=1), GROUP)
    terms_a = gate_up_terms(order, x_a, far_a, swap(x_a, "c"), swap(far_a, "c"), w_in, w_in_other, nz * n, 0)
    rest = after(rest, *terms_a)
    inverse = from_row(rest[:, 2 * n], CAP).reshape(EXPERTS, 3, n).transpose(1, 0, 2).reshape(3 * group)
    near = jnp.concatenate(
        [rest[:, :n].reshape(group, feat), rest[:, n : 2 * n].reshape(group, feat), as_rows(inverse, feat)], axis=0
    )
    near = all_to_all(jnp.broadcast_to(near[None], (nz,) + near.shape), "z").reshape((nz,) + near.shape)

    def over_yl(parts):
        return [parts[0]] + [lax.ppermute(parts[i], "yl", Y_XOR[i]) for i in range(1, 4)]

    def hidden_of(parts, inverse):
        full = sum(p.astype(F32) for p in parts) * inverse[:, None]
        return (jax.nn.silu(full[:, :half]) * full[:, half:]).astype(BF16)

    def to_xl(down):
        return down[0], swap(down[1], "xl")

    def total(stay, came):
        return (stay.astype(F32) + came.astype(F32)).astype(BF16)

    sums_a = over_yl(terms_a)
    near = after(near, *sums_a[1:])
    tail = near[:, 2 * group :, : 9 * group + 96]
    tails = (tail, swap(tail, "xl"))
    inverse = jnp.stack([from_row(t[:, 0], 3 * group).reshape(nz, 3, EXPERTS, n) for t in tails])
    inverse_a = inverse[:, :, 0].transpose(0, 2, 1, 3).reshape(4, rows // 2)
    inverse_bc = inverse[:, :, 1:].transpose(2, 0, 1, 3, 4).reshape(2, 4, rows // 2)

    def own(v):
        return lax.dynamic_index_in_dim(v, me, 0, keepdims=False)

    far = swap(near, "xl")
    near_other = swap(near, "c")
    hidden_a = over_yl([hidden_of(sums_a, own(inverse_a))] * 4)
    far = after(far, *hidden_a)
    far_other = swap(far, "c")
    terms_b = gate_up_terms(order, near, far, near_other, far_other, w_in, w_in_other, group, 0)
    hid = jnp.concatenate(hidden_a, axis=0)
    down_a = down_terms(order, hid, swap(hid, "c"), w_down)
    stay_a, came_a = to_xl(down_a)
    sums_b = over_yl(terms_b)
    terms_c = gate_up_terms(
        order, near, far, near_other, after(far_other, *terms_b), w_in, w_in_other, group, 1
    )
    sums_b[1] = after(sums_b[1], *down_a)
    came_a = after(came_a, *sums_b[1:])
    back_a = all_to_all(total(stay_a, came_a).reshape(-1, n, feat), ROUTE)
    hidden_b = over_yl([hidden_of(sums_b, own(inverse_bc[0]))] * 4)
    sums_c = over_yl(terms_c)
    hid = jnp.concatenate(hidden_b, axis=0)
    down_b = down_terms(order, hid, swap(hid, "c"), w_down)
    stay_b, came_b = to_xl(down_b)
    back_a = after(back_a, *sums_c[1:])
    hidden_c = over_yl([hidden_of(sums_c, own(inverse_bc[1]))] * 4)
    hid = jnp.concatenate(hidden_c, axis=0)
    came_b = after(came_b, hid)
    down_c = down_terms(order, hid, swap(hid, "c"), w_down)

    def give_back(stay, came):
        both = total(stay, came).reshape(nz, EXPERTS, n, feat).transpose(1, 0, 2, 3).reshape(-1, n, feat)
        return all_to_all(both, ROUTE)

    def over_z(back):
        return jnp.sum(back.reshape(EXPERTS, nz, n, feat).astype(F32), axis=1).astype(BF16)

    back_b = give_back(stay_b, came_b)
    back_c = give_back(*to_xl(down_c))
    returned = jnp.concatenate([over_z(back_a), over_z(after(back_b, down_c[0])), over_z(back_c)], axis=1)
    moe_rows = jnp.einsum("ect,ecd->td", select, returned, preferred_element_type=F32)
    return (route_weight[:, None] * moe_rows).astype(BF16)


def solution(mesh):
    fine = Mesh(mesh.devices.reshape(2, 2, 2, 8, 4, 2), CTX + EXP)
    wide = P(CTX, EXP)
    in_specs = (wide, wide, wide, wide, P(EXP), P(CTX, None), P(CTX), wide, wide, wide)
    return jax.shard_map(body, mesh=fine, in_specs=in_specs, out_specs=wide, check_vma=False)
```

```python
import math
from functools import partial

import jax
import jax.numpy as jnp
from jax import lax
from jax.experimental import pallas as pl
from jax.experimental.pallas import tpu as pltpu
from jax.sharding import Mesh, PartitionSpec as P

D = 6144
HD = 128
EXPERTS = 4
CAP = 24
F32 = jnp.float32
BF16 = jnp.bfloat16

CTX = ("yh", "xh", "xl", "z")
EXP = ("yl", "c")
HALF = ("xh", "xl", "z")
GROUP = ("yh", "xh", "xl")
SWAP = [(0, 1), (1, 0)]
Y_XOR = [[(i, i ^ k) for i in range(4)] for k in range(4)]


def swap(x, axis):
    return lax.ppermute(x, axis, SWAP)


def split3(v):
    hi = lax.reduce_precision(v, 8, 7)
    mid = lax.reduce_precision(v - hi, 8, 7)
    lo = (v - hi) - mid
    return [p.astype(BF16) for p in (hi, mid, lo)]


def attend(queries, keys, values, early):
    rows = queries.shape[0]
    heads = queries.shape[1] // HD
    yh = lax.axis_index("yh")
    scale = 1.0 / math.sqrt(HD)

    foreign = lax.ppermute(queries, "yh", [(1, 0)])
    kv = jnp.concatenate([keys, values], axis=1)
    members = lax.axis_size(HALF)
    kv = lax.all_to_all(
        jnp.broadcast_to(kv[None], (members,) + kv.shape), HALF, split_axis=0, concat_axis=0, tiled=True
    ).reshape(members * rows, 2 * HD)
    kv, *early = lax.optimization_barrier((kv,) + early)
    k_all, v_all = kv[:, :HD], kv[:, HD:]
    count = members * rows

    def stacked(q):
        return q.reshape(rows, heads, HD).transpose(1, 0, 2).reshape(heads * rows, HD)

    q_all = jnp.concatenate([stacked(queries), stacked(foreign)], axis=0)
    own_pos = lax.axis_index(HALF) * rows + jnp.tile(jnp.arange(rows, dtype=jnp.int32), heads)
    limit = jnp.concatenate([own_pos, jnp.full_like(own_pos, count)])
    scores = jnp.einsum("qd,kd->qk", q_all, k_all, preferred_element_type=F32) * scale
    allowed = jnp.arange(count, dtype=jnp.int32)[None, :] <= limit[:, None]
    scores = jnp.where(allowed, scores, -1e30)
    top = jnp.max(scores, axis=1)
    weights = jnp.exp(scores - top[:, None])
    total = jnp.sum(weights, axis=1)
    acc = jnp.einsum("qk,kd->qd", weights.astype(BF16), v_all, preferred_element_type=F32)
    out = acc / total[:, None]
    lse = top + jnp.log(total)

    n = heads * rows

    def unstacked(o):
        return o.reshape(heads, rows, HD).transpose(1, 0, 2).reshape(rows, heads * HD)

    out_own, out_far = unstacked(out[:n]), unstacked(out[n:])
    lse_own, lse_far = lse[:n].reshape(heads, rows).T, lse[n:].reshape(heads, rows).T
    tail = jnp.concatenate(split3(lse_far), axis=1)
    tail = jnp.pad(tail, ((0, 0), (0, HD - tail.shape[1])))
    message = jnp.concatenate([out_far.astype(BF16), tail], axis=1)
    got = lax.ppermute(message, "yh", [(0, 1)])
    got_out = got[:, : heads * HD].astype(F32)
    parts = got[:, heads * HD : heads * HD + 3 * heads].astype(F32)
    got_lse = parts[:, :heads] + parts[:, heads : 2 * heads] + parts[:, 2 * heads :]
    share = jnp.where(yh == 1, jax.nn.sigmoid(got_lse - lse_own), 0.0)
    share = jnp.repeat(share, HD, axis=1)
    return (out_own * (1.0 - share) + got_out * share).astype(BF16), early


def expand(order_ref, x_ref, o_ref, w_ref, wo_ref, *rest):
    out_refs, acc_ref = rest[:4], rest[4]
    contract = (((1,), (1,)), ((), ()))
    x, o = (r[...].reshape(acc_ref.shape[0], r.shape[-1]) for r in (x_ref, o_ref))
    acc_ref[...] = lax.dot_general(x, w_ref[...], contract, preferred_element_type=F32) + lax.dot_general(
        o, wo_ref[...], contract, preferred_element_type=F32
    )
    share = out_refs[0].shape[0]
    for i, ref in enumerate(out_refs):
        at = pl.multiple_of((order_ref[0] ^ i) * share, share)
        ref[...] = acc_ref[pl.ds(at, share), :].astype(BF16)


def gate_up_terms(order, x, other, w, wo, block):
    hidden, feat = w.shape
    cols = hidden // 2
    rows = x.shape[0] * block
    share = rows // 4
    spec = pl.BlockSpec((x.shape[0], block, feat), lambda n, o: (0, 0, 0))
    weight = pl.BlockSpec((cols, feat), lambda n, o: (n, 0))
    out = pl.BlockSpec((share, cols), lambda n, o: (0, n))
    shape = pltpu.HBM((share, hidden), BF16)
    return pl.pallas_call(
        expand,
        grid_spec=pltpu.PrefetchScalarGridSpec(
            num_scalar_prefetch=1,
            grid=(2,),
            in_specs=[spec, spec, weight, weight],
            out_specs=[out] * 4,
            scratch_shapes=[pltpu.VMEM((rows, cols), F32)],
        ),
        out_shape=[shape] * 4,
        cost_estimate=pl.CostEstimate(
            flops=4 * rows * hidden * feat, transcendentals=0, bytes_accessed=4 * hidden * feat + 2 * rows * hidden
        ),
        compiler_params=pltpu.CompilerParams(vmem_limit_bytes=40 << 20),
        name="gate_up_terms",
    )(order, x, other, w, wo)


def contract_hidden(order_ref, h_ref, ho_ref, w_ref, out_ref):
    core = order_ref[1]
    half = w_ref.shape[0] // 2
    own = pl.multiple_of(core * half, half)
    other = pl.multiple_of((1 - core) * half, half)
    acc = jnp.dot(h_ref[...], w_ref[pl.ds(own, half), :], preferred_element_type=F32)
    acc += jnp.dot(ho_ref[...], w_ref[pl.ds(other, half), :], preferred_element_type=F32)
    share = h_ref.shape[0] // 4
    for i in range(4):
        at = pl.multiple_of((order_ref[0] ^ i) * share, share)
        out_ref[pl.ds(at, share), :] = acc[i * share : (i + 1) * share].astype(BF16)


def down_terms(order, h, ho, w):
    rows = h.shape[0]
    hidden, feat = w.shape
    whole = pl.BlockSpec(memory_space=pltpu.VMEM)
    return pl.pallas_call(
        contract_hidden,
        in_specs=[pl.BlockSpec(memory_space=pltpu.SMEM), whole, whole, whole],
        out_specs=whole,
        out_shape=jax.ShapeDtypeStruct((rows, feat), BF16),
        cost_estimate=pl.CostEstimate(
            flops=2 * rows * hidden * feat, transcendentals=0, bytes_accessed=2 * hidden * feat + 4 * rows * hidden
        ),
        compiler_params=pltpu.CompilerParams(vmem_limit_bytes=40 << 20),
        name="down_terms",
    )(order, h, ho, w)


def after(value, *others):
    return lax.optimization_barrier((value,) + others)[0]


def as_rows(v, feat):
    row = jnp.concatenate(split3(v), axis=-1)
    return jnp.pad(row[..., None, :], [(0, 0)] * (v.ndim - 1) + [(0, 7), (0, feat - row.shape[-1])])


def from_row(row, n):
    hi, mid, lo = (row[..., k * n : (k + 1) * n].astype(F32) for k in range(3))
    return hi + mid + lo


def body(queries, keys, values, residual, norm_gain, routes, route_weight, w_gate, w_up, w_down):
    feat = residual.shape[1]
    half = w_gate.shape[0] // 2
    core = lax.axis_index("c")
    me = lax.axis_index("yl")
    order = jnp.stack([me, core]).astype(jnp.int32)

    def halves(which):
        cut = partial(lax.dynamic_slice_in_dim, start_index=which * half, slice_size=half, axis=0)
        return jnp.concatenate([cut(w_gate), cut(w_up)], axis=0)

    w_in = halves(core)
    w_in_other = swap(halves(1 - core), "c")

    chosen = routes[:, 0]
    expert_ids = jnp.arange(EXPERTS, dtype=jnp.int32)
    onehot = (chosen[:, None] == expert_ids[None, :]).astype(jnp.int32)
    slot_index = jnp.sum((jnp.cumsum(onehot, axis=0) - 1) * onehot, axis=1)
    slot_ids = jnp.arange(CAP, dtype=jnp.int32)
    taken = (chosen[None, None, :] == expert_ids[:, None, None]) & (
        slot_index[None, None, :] == slot_ids[None, :, None]
    )
    select = taken.astype(BF16)

    attn, (w_in, w_in_other) = attend(queries, keys, values, (w_in, w_in_other))
    mixed = residual.astype(F32) + attn.astype(F32)
    squares = jnp.sum(mixed * mixed, axis=1)
    packed = jnp.einsum(
        "ect,td->ecd", select, (mixed * norm_gain[None, :]).astype(BF16), preferred_element_type=F32
    ).astype(BF16)

    nz = lax.axis_size("z")
    sources = EXPERTS * lax.axis_size("xl")
    n = CAP // 2
    block = sources * n

    def all_to_all(x, axes):
        return lax.all_to_all(x, axes, split_axis=0, concat_axis=0, tiled=True)

    def along_z(x):
        return all_to_all(jnp.broadcast_to(x[None], (nz,) + x.shape), "z").reshape((nz,) + x.shape)

    squares = jnp.sum(jnp.where(taken, squares[None, None, :], 0.0), axis=2)
    rows = jnp.concatenate([packed, as_rows(squares, feat)], axis=1)
    rows = jnp.broadcast_to(rows[:, None], (EXPERTS, 2) + rows.shape[1:]).reshape(sources, CAP + 8, feat)
    rows = all_to_all(rows, GROUP)
    part_a, part_b = (rows[:, k * n : (k + 1) * n].reshape(block, feat) for k in range(2))
    x_a = along_z(part_a)
    squares = from_row(rows[:, CAP], CAP).reshape(sources, 2, n).transpose(1, 0, 2).reshape(2 * block)
    inverse = lax.rsqrt(lax.psum(squares, EXP) / D + 1e-05)
    x_a, inverse = lax.optimization_barrier((x_a, inverse))
    x_b = along_z(jnp.concatenate([part_b, as_rows(inverse, feat)], axis=0))

    def over_yl(parts):
        return [parts[0]] + [lax.ppermute(parts[i], "yl", Y_XOR[i]) for i in range(1, 4)]

    def hidden_of(parts, inverse):
        inverse = lax.dynamic_index_in_dim(inverse.reshape(4, -1), me, 0, keepdims=False)
        full = sum(p.astype(F32) for p in parts) * inverse[:, None]
        return (jax.nn.silu(full[:, :half]) * full[:, half:]).astype(BF16)

    def down_of(parts):
        hid = jnp.concatenate(parts, axis=0)
        return down_terms(order, hid, swap(hid, "c"), w_down)

    def give_back(down):
        return all_to_all(down.reshape(nz, block, feat), "z")

    def over_z(back):
        return jnp.sum(back.astype(F32), axis=0).astype(BF16).reshape(sources, n, feat)

    terms_a = gate_up_terms(order, x_a, swap(x_a, "c"), w_in, w_in_other, block)
    sums_a = over_yl(terms_a)
    x_b = after(x_b, *sums_a[1:])
    inverse = from_row(x_b[:, block], 2 * block)
    hidden_a = hidden_of(sums_a, inverse[:, :block])
    x_b = after(x_b, hidden_a)
    hids_a = over_yl([hidden_a] * 4)
    terms_b = gate_up_terms(order, x_b, swap(x_b, "c"), w_in, w_in_other, block)
    hids_a[1] = after(hids_a[1], *terms_b)
    sums_b = over_yl(terms_b)
    down_a = down_of(hids_a)
    back_a = give_back(down_a)
    sums_b[1] = after(sums_b[1], down_a)
    hids_b = over_yl([hidden_of(sums_b, inverse[:, block:])] * 4)
    back_a = after(back_a, *hids_b[1:])
    back_b = give_back(down_of(hids_b))
    returned = all_to_all(jnp.concatenate([over_z(back_a), over_z(back_b)], axis=1), GROUP)
    returned = jnp.sum(returned.reshape(EXPERTS, 2, CAP, feat).astype(F32), axis=1)
    moe_rows = jnp.einsum(
        "ect,ecd->td", taken.astype(F32), returned, precision=lax.Precision.HIGHEST, preferred_element_type=F32
    )
    return (route_weight[:, None] * moe_rows).astype(BF16)


def solution(mesh):
    fine = Mesh(mesh.devices.reshape(2, 2, 2, 8, 4, 2), CTX + EXP)
    wide = P(CTX, EXP)
    in_specs = (wide, wide, wide, wide, P(EXP), P(CTX, None), P(CTX), wide, wide, wide)
    return jax.shard_map(body, mesh=fine, in_specs=in_specs, out_specs=wide, check_vma=False)
```

```python
import math
from functools import partial

import jax
import jax.numpy as jnp
from jax import lax
from jax.experimental import pallas as pl
from jax.experimental.pallas import tpu as pltpu
from jax.sharding import Mesh, PartitionSpec as P

D = 6144
HD = 128
EXPERTS = 4
CAP = 24
F32 = jnp.float32
BF16 = jnp.bfloat16

CTX = ("yh", "xh", "xl", "z")
EXP = ("yl", "c")
HALF = ("xh", "xl", "z")
GROUP = ("yh", "xh", "xl")
SWAP = [(0, 1), (1, 0)]
Y_XOR = [[(i, i ^ k) for i in range(4)] for k in range(4)]


def swap(x, axis):
    return lax.ppermute(x, axis, SWAP)


def split3(v):
    hi = lax.reduce_precision(v, 8, 7)
    mid = lax.reduce_precision(v - hi, 8, 7)
    lo = (v - hi) - mid
    return [p.astype(BF16) for p in (hi, mid, lo)]


def softmax_block(base_ref, own_ref, far_ref, kv_ref, out_ref, lse_ref, message_ref):
    rows = own_ref.shape[0]
    count = kv_ref.shape[0]
    heads = own_ref.shape[1] // HD
    scale = 1.0 / math.sqrt(HD)
    keys, values = kv_ref[:, :HD], kv_ref[:, HD:]
    limit = base_ref[0] + lax.broadcasted_iota(jnp.int32, (rows, count), 0)
    allowed = lax.broadcasted_iota(jnp.int32, (rows, count), 1) <= limit
    lane = lax.broadcasted_iota(jnp.int32, (rows, HD), 1)
    tail = jnp.zeros((rows, HD), F32)
    for h in range(heads):
        cols = slice(h * HD, (h + 1) * HD)
        for far, ref in ((False, own_ref), (True, far_ref)):
            dots = lax.dot_general(ref[:, cols], keys, (((1,), (1,)), ((), ())), preferred_element_type=F32)
            if not far:
                dots = jnp.where(allowed, dots, -1e30)
            top = jnp.max(dots, axis=1, keepdims=True)
            weights = jnp.exp2((dots - top) * (scale * math.log2(math.e)))
            total = jnp.sum(weights, axis=1, keepdims=True)
            acc = jnp.dot(weights.astype(BF16), values, preferred_element_type=F32)
            out = acc / total
            lse = top * scale + jnp.log(total)
            if far:
                message_ref[:, cols] = out.astype(BF16)
                hi = lse.astype(BF16).astype(F32)
                mid = (lse - hi).astype(BF16).astype(F32)
                for k, part in enumerate((hi, mid, lse - hi - mid)):
                    tail = jnp.where(lane == k * heads + h, part, tail)
            else:
                out_ref[:, cols] = out
                lse_ref[:, cols] = jnp.broadcast_to(lse, (rows, HD))
    message_ref[:, heads * HD :] = tail.astype(BF16)


def attend(queries, keys, values, early):
    rows, width = queries.shape
    heads = width // HD
    yh = lax.axis_index("yh")
    foreign = lax.ppermute(queries, "yh", [(1, 0)])
    kv = jnp.concatenate([keys, values], axis=1)
    members = lax.axis_size(HALF)
    kv = lax.all_to_all(
        jnp.broadcast_to(kv[None], (members,) + kv.shape), HALF, split_axis=0, concat_axis=0, tiled=True
    ).reshape(members * rows, 2 * HD)
    kv, *early = lax.optimization_barrier((kv,) + early)
    whole = pl.BlockSpec(memory_space=pltpu.VMEM)
    out, lse, message = pl.pallas_call(
        softmax_block,
        in_specs=[pl.BlockSpec(memory_space=pltpu.SMEM), whole, whole, whole],
        out_specs=[whole, whole, whole],
        out_shape=[
            jax.ShapeDtypeStruct((rows, width), F32),
            jax.ShapeDtypeStruct((rows, width), F32),
            jax.ShapeDtypeStruct((rows, width + HD), BF16),
        ],
        cost_estimate=pl.CostEstimate(
            flops=8 * rows * width * members * rows,
            transcendentals=2 * rows * heads * members * rows,
            bytes_accessed=4 * members * rows * HD + 16 * rows * width,
        ),
        compiler_params=pltpu.CompilerParams(vmem_limit_bytes=48 << 20),
        name="softmax_block",
    )((lax.axis_index(HALF) * rows).astype(jnp.int32).reshape(1), queries, foreign, kv)
    got = lax.ppermute(message, "yh", [(0, 1)])
    parts = got[:, width : width + 3 * heads].astype(F32)
    got_lse = parts[:, :heads] + parts[:, heads : 2 * heads] + parts[:, 2 * heads :]
    share = jnp.where(yh == 1, jax.nn.sigmoid(jnp.repeat(got_lse, HD, axis=1) - lse), 0.0)
    return (out * (1.0 - share) + got[:, :width].astype(F32) * share).astype(BF16), early


def expand(order_ref, x_ref, o_ref, w_ref, wo_ref, *rest):
    out_refs, acc_ref = rest[:4], rest[4]
    contract = (((1,), (1,)), ((), ()))
    x, o = (r[...].reshape(acc_ref.shape[0], r.shape[-1]) for r in (x_ref, o_ref))
    acc_ref[...] = lax.dot_general(x, w_ref[...], contract, preferred_element_type=F32) + lax.dot_general(
        o, wo_ref[...], contract, preferred_element_type=F32
    )
    share = out_refs[0].shape[0]
    for i, ref in enumerate(out_refs):
        at = pl.multiple_of((order_ref[0] ^ i) * share, share)
        ref[...] = acc_ref[pl.ds(at, share), :].astype(BF16)


def gate_up_terms(order, x, other, w, wo, block):
    hidden, feat = w.shape
    cols = hidden // 2
    rows = x.shape[0] * block
    share = rows // 4
    spec = pl.BlockSpec((x.shape[0], block, feat), lambda n, o: (0, 0, 0))
    weight = pl.BlockSpec((cols, feat), lambda n, o: (n, 0))
    out = pl.BlockSpec((share, cols), lambda n, o: (0, n))
    shape = pltpu.HBM((share, hidden), BF16)
    return pl.pallas_call(
        expand,
        grid_spec=pltpu.PrefetchScalarGridSpec(
            num_scalar_prefetch=1,
            grid=(2,),
            in_specs=[spec, spec, weight, weight],
            out_specs=[out] * 4,
            scratch_shapes=[pltpu.VMEM((rows, cols), F32)],
        ),
        out_shape=[shape] * 4,
        cost_estimate=pl.CostEstimate(
            flops=4 * rows * hidden * feat, transcendentals=0, bytes_accessed=4 * hidden * feat + 2 * rows * hidden
        ),
        compiler_params=pltpu.CompilerParams(vmem_limit_bytes=40 << 20),
        name="gate_up_terms",
    )(order, x, other, *(pltpu.with_memory_space_constraint(v, pltpu.HBM) for v in (w, wo)))


def contract_hidden(order_ref, h_ref, ho_ref, w_ref, out_ref):
    core = order_ref[1]
    half = w_ref.shape[0] // 2
    own = pl.multiple_of(core * half, half)
    other = pl.multiple_of((1 - core) * half, half)
    acc = jnp.dot(h_ref[...], w_ref[pl.ds(own, half), :], preferred_element_type=F32)
    acc += jnp.dot(ho_ref[...], w_ref[pl.ds(other, half), :], preferred_element_type=F32)
    share = h_ref.shape[0] // 4
    for i in range(4):
        at = pl.multiple_of((order_ref[0] ^ i) * share, share)
        out_ref[pl.ds(at, share), :] = acc[i * share : (i + 1) * share].astype(BF16)


def down_terms(order, h, ho, w):
    rows = h.shape[0]
    hidden, feat = w.shape
    whole = pl.BlockSpec(memory_space=pltpu.VMEM)
    return pl.pallas_call(
        contract_hidden,
        in_specs=[pl.BlockSpec(memory_space=pltpu.SMEM), whole, whole, whole],
        out_specs=whole,
        out_shape=jax.ShapeDtypeStruct((rows, feat), BF16),
        cost_estimate=pl.CostEstimate(
            flops=2 * rows * hidden * feat, transcendentals=0, bytes_accessed=2 * hidden * feat + 4 * rows * hidden
        ),
        compiler_params=pltpu.CompilerParams(vmem_limit_bytes=40 << 20),
        name="down_terms",
    )(order, h, ho, w)


def after(value, *others):
    return lax.optimization_barrier((value,) + others)[0]


def as_rows(v, feat):
    row = jnp.concatenate(split3(v), axis=-1)
    return jnp.pad(row[..., None, :], [(0, 0)] * (v.ndim - 1) + [(0, 7), (0, feat - row.shape[-1])])


def from_row(row, n):
    hi, mid, lo = (row[..., k * n : (k + 1) * n].astype(F32) for k in range(3))
    return hi + mid + lo


def body(queries, keys, values, residual, norm_gain, routes, route_weight, w_gate, w_up, w_down):
    feat = residual.shape[1]
    half = w_gate.shape[0] // 2
    core = lax.axis_index("c")
    me = lax.axis_index("yl")
    order = jnp.stack([me, core]).astype(jnp.int32)

    def halves(which):
        cut = partial(lax.dynamic_slice_in_dim, start_index=which * half, slice_size=half, axis=0)
        return jnp.concatenate([cut(w_gate), cut(w_up)], axis=0)

    w_in = halves(core)
    w_in_other = swap(halves(1 - core), "c")

    chosen = routes[:, 0]
    expert_ids = jnp.arange(EXPERTS, dtype=jnp.int32)
    onehot = (chosen[:, None] == expert_ids[None, :]).astype(jnp.int32)
    slot_index = jnp.sum((jnp.cumsum(onehot, axis=0) - 1) * onehot, axis=1)
    slot_ids = jnp.arange(CAP, dtype=jnp.int32)
    taken = (chosen[None, None, :] == expert_ids[:, None, None]) & (
        slot_index[None, None, :] == slot_ids[None, :, None]
    )
    select = taken.astype(BF16)

    attn, (w_in, w_in_other) = attend(queries, keys, values, (w_in, w_in_other))
    mixed = residual.astype(F32) + attn.astype(F32)
    squares = jnp.sum(mixed * mixed, axis=1)
    packed = jnp.einsum(
        "ect,td->ecd", select, (mixed * norm_gain[None, :]).astype(BF16), preferred_element_type=F32
    ).astype(BF16)

    nz = lax.axis_size("z")
    sources = EXPERTS * lax.axis_size("xl")
    n = CAP // 2
    block = sources * n

    def all_to_all(x, axes):
        return lax.all_to_all(x, axes, split_axis=0, concat_axis=0, tiled=True)

    def along_z(x):
        return all_to_all(jnp.broadcast_to(x[None], (nz,) + x.shape), "z").reshape((nz,) + x.shape)

    squares = jnp.sum(jnp.where(taken, squares[None, None, :], 0.0), axis=2)
    rows = jnp.concatenate([packed, as_rows(squares, feat)], axis=1)
    rows = jnp.broadcast_to(rows[:, None], (EXPERTS, 2) + rows.shape[1:]).reshape(sources, CAP + 8, feat)
    rows = all_to_all(rows, GROUP)
    part_a, part_b = (rows[:, k * n : (k + 1) * n].reshape(block, feat) for k in range(2))
    x_a = along_z(part_a)
    squares = from_row(rows[:, CAP], CAP).reshape(sources, 2, n).transpose(1, 0, 2).reshape(2 * block)
    inverse = lax.rsqrt(lax.psum(squares, EXP) / D + 1e-05)
    x_a, inverse = lax.optimization_barrier((x_a, inverse))
    x_b = along_z(jnp.concatenate([part_b, as_rows(inverse, feat)], axis=0))

    def over_yl(parts):
        return [parts[0]] + [lax.ppermute(parts[i], "yl", Y_XOR[i]) for i in range(1, 4)]

    def hidden_of(parts, inverse):
        inverse = lax.dynamic_index_in_dim(inverse.reshape(4, -1), me, 0, keepdims=False)
        full = sum(p.astype(F32) for p in parts) * inverse[:, None]
        return (jax.nn.silu(full[:, :half]) * full[:, half:]).astype(BF16)

    def down_of(parts):
        hid = jnp.concatenate(parts, axis=0)
        return down_terms(order, hid, swap(hid, "c"), w_down)

    def give_back(down):
        return all_to_all(down.reshape(nz, block, feat), "z")

    def over_z(back):
        return jnp.sum(back.astype(F32), axis=0).astype(BF16).reshape(sources, n, feat)

    terms_a = gate_up_terms(order, x_a, swap(x_a, "c"), w_in, w_in_other, block)
    sums_a = over_yl(terms_a)
    x_b = after(x_b, sums_a[3])
    inverse = from_row(x_b[:, block], 2 * block)
    terms_b = gate_up_terms(order, x_b, swap(x_b, "c"), w_in, w_in_other, block)
    sums_a[1] = after(sums_a[1], *terms_b)
    hids_a = over_yl([hidden_of(sums_a, inverse[:, :block])] * 4)
    sums_b = over_yl(terms_b)
    hids_a[1] = after(hids_a[1], sums_b[3])
    down_a = down_of(hids_a)
    back_a = give_back(down_a)
    sums_b[1] = after(sums_b[1], down_a)
    hids_b = over_yl([hidden_of(sums_b, inverse[:, block:])] * 4)
    back_a = after(back_a, *hids_b[1:])
    back_b = give_back(down_of(hids_b))
    returned = all_to_all(jnp.concatenate([over_z(back_a), over_z(back_b)], axis=1), GROUP)
    returned = jnp.sum(returned.reshape(EXPERTS, 2, CAP, feat).astype(F32), axis=1)
    moe_rows = jnp.einsum(
        "ect,ecd->td", taken.astype(F32), returned, precision=lax.Precision.HIGHEST, preferred_element_type=F32
    )
    return (route_weight[:, None] * moe_rows).astype(BF16)


def solution(mesh):
    fine = Mesh(mesh.devices.reshape(2, 2, 2, 8, 4, 2), CTX + EXP)
    wide = P(CTX, EXP)
    in_specs = (wide, wide, wide, wide, P(EXP), P(CTX, None), P(CTX), wide, wide, wide)
    return jax.shard_map(body, mesh=fine, in_specs=in_specs, out_specs=wide, check_vma=False)
```

```python
import math
from functools import partial

import jax
import jax.numpy as jnp
from jax import lax
from jax.experimental import pallas as pl
from jax.experimental.pallas import tpu as pltpu
from jax.sharding import Mesh, PartitionSpec as P

D = 6144
HD = 128
EXPERTS = 4
CAP = 24
F32 = jnp.float32
BF16 = jnp.bfloat16

CTX = ("yh", "xh", "xl", "z")
EXP = ("yl", "c")
HALF = ("xh", "xl", "z")
GROUP = ("yh", "xh", "xl")
SWAP = [(0, 1), (1, 0)]
Y_XOR = [[(i, i ^ k) for i in range(4)] for k in range(4)]


def swap(x, axis):
    return lax.ppermute(x, axis, SWAP)


def split3(v):
    hi = lax.reduce_precision(v, 8, 7)
    mid = lax.reduce_precision(v - hi, 8, 7)
    lo = (v - hi) - mid
    return [p.astype(BF16) for p in (hi, mid, lo)]


def softmax_block(base_ref, own_ref, far_ref, kv_ref, out_ref, lse_ref, message_ref):
    rows = own_ref.shape[0]
    count = kv_ref.shape[0]
    heads = own_ref.shape[1] // HD
    scale = 1.0 / math.sqrt(HD)
    keys, values = kv_ref[:, :HD], kv_ref[:, HD:]
    limit = base_ref[0] + lax.broadcasted_iota(jnp.int32, (rows, count), 0)
    allowed = lax.broadcasted_iota(jnp.int32, (rows, count), 1) <= limit
    lane = lax.broadcasted_iota(jnp.int32, (rows, HD), 1)
    tail = jnp.zeros((rows, HD), F32)
    for h in range(heads):
        cols = slice(h * HD, (h + 1) * HD)
        for far, ref in ((False, own_ref), (True, far_ref)):
            dots = lax.dot_general(ref[:, cols], keys, (((1,), (1,)), ((), ())), preferred_element_type=F32)
            if not far:
                dots = jnp.where(allowed, dots, -1e30)
            top = jnp.max(dots, axis=1, keepdims=True)
            weights = jnp.exp2((dots - top) * (scale * math.log2(math.e)))
            total = jnp.sum(weights, axis=1, keepdims=True)
            acc = jnp.dot(weights.astype(BF16), values, preferred_element_type=F32)
            out = acc / total
            lse = top * scale + jnp.log(total)
            if far:
                message_ref[:, cols] = out.astype(BF16)
                hi = lse.astype(BF16).astype(F32)
                mid = (lse - hi).astype(BF16).astype(F32)
                for k, part in enumerate((hi, mid, lse - hi - mid)):
                    tail = jnp.where(lane == k * heads + h, part, tail)
            else:
                out_ref[:, cols] = out
                lse_ref[:, cols] = jnp.broadcast_to(lse, (rows, HD))
    message_ref[:, heads * HD :] = tail.astype(BF16)


def attend(queries, keys, values, early):
    rows, width = queries.shape
    heads = width // HD
    yh = lax.axis_index("yh")
    foreign = lax.ppermute(queries, "yh", [(1, 0)])
    kv = jnp.concatenate([keys, values], axis=1)
    members = lax.axis_size(HALF)
    kv = lax.all_to_all(
        jnp.broadcast_to(kv[None], (members,) + kv.shape), HALF, split_axis=0, concat_axis=0, tiled=True
    ).reshape(members * rows, 2 * HD)
    kv, *early = lax.optimization_barrier((kv,) + early)
    whole = pl.BlockSpec(memory_space=pltpu.VMEM)
    out, lse, message = pl.pallas_call(
        softmax_block,
        in_specs=[pl.BlockSpec(memory_space=pltpu.SMEM), whole, whole, whole],
        out_specs=[whole, whole, whole],
        out_shape=[
            jax.ShapeDtypeStruct((rows, width), F32),
            jax.ShapeDtypeStruct((rows, width), F32),
            jax.ShapeDtypeStruct((rows, width + HD), BF16),
        ],
        cost_estimate=pl.CostEstimate(
            flops=8 * rows * width * members * rows,
            transcendentals=2 * rows * heads * members * rows,
            bytes_accessed=4 * members * rows * HD + 16 * rows * width,
        ),
        compiler_params=pltpu.CompilerParams(vmem_limit_bytes=48 << 20),
        name="softmax_block",
    )((lax.axis_index(HALF) * rows).astype(jnp.int32).reshape(1), queries, foreign, kv)
    got = lax.ppermute(message, "yh", [(0, 1)])
    parts = got[:, width : width + 3 * heads].astype(F32)
    got_lse = parts[:, :heads] + parts[:, heads : 2 * heads] + parts[:, 2 * heads :]
    share = jnp.where(yh == 1, jax.nn.sigmoid(jnp.repeat(got_lse, HD, axis=1) - lse), 0.0)
    return (out * (1.0 - share) + got[:, :width].astype(F32) * share).astype(BF16), early


def expand(order_ref, x_ref, o_ref, w_ref, wo_ref, *rest):
    keep_ref, pair_ref, send_ref, acc_ref = rest
    contract = (((1,), (1,)), ((), ()))
    x, o = (r[...].reshape(acc_ref.shape[0], r.shape[-1]) for r in (x_ref, o_ref))
    acc_ref[...] = lax.dot_general(x, w_ref[...], contract, preferred_element_type=F32) + lax.dot_general(
        o, wo_ref[...], contract, preferred_element_type=F32
    )
    share = keep_ref.shape[0]
    for i, ref in enumerate((keep_ref, send_ref.at[:share], pair_ref, send_ref.at[share:])):
        at = pl.multiple_of((order_ref[0] ^ i) * share, share)
        ref[...] = acc_ref[pl.ds(at, share), :].astype(BF16)


def gate_up_terms(order, x, other, w, wo, block):
    hidden, feat = w.shape
    cols = hidden // 2
    rows = x.shape[0] * block
    share = rows // 4
    spec = pl.BlockSpec((x.shape[0], block, feat), lambda n, o: (0, 0, 0))
    weight = pl.BlockSpec((cols, feat), lambda n, o: (n, 0))
    blocks = (share, share, 2 * share)
    return pl.pallas_call(
        expand,
        grid_spec=pltpu.PrefetchScalarGridSpec(
            num_scalar_prefetch=1,
            grid=(2,),
            in_specs=[spec, spec, weight, weight],
            out_specs=[pl.BlockSpec((b, cols), lambda n, o: (0, n)) for b in blocks],
            scratch_shapes=[pltpu.VMEM((rows, cols), F32)],
        ),
        out_shape=[pltpu.HBM((b, hidden), BF16) for b in blocks],
        cost_estimate=pl.CostEstimate(
            flops=4 * rows * hidden * feat, transcendentals=0, bytes_accessed=4 * hidden * feat + 2 * rows * hidden
        ),
        compiler_params=pltpu.CompilerParams(vmem_limit_bytes=40 << 20),
        name="gate_up_terms",
    )(order, x, other, *(pltpu.with_memory_space_constraint(v, pltpu.HBM) for v in (w, wo)))


def contract_hidden(order_ref, h_ref, ho_ref, w_ref, out_ref):
    core = order_ref[1]
    half = w_ref.shape[0] // 2
    own = pl.multiple_of(core * half, half)
    other = pl.multiple_of((1 - core) * half, half)
    acc = jnp.dot(h_ref[...], w_ref[pl.ds(own, half), :], preferred_element_type=F32)
    acc += jnp.dot(ho_ref[...], w_ref[pl.ds(other, half), :], preferred_element_type=F32)
    share = h_ref.shape[0] // 4
    for k, i in enumerate((0, 2, 1, 3)):
        at = pl.multiple_of((order_ref[0] ^ i) * share, share)
        out_ref[pl.ds(at, share), :] = acc[k * share : (k + 1) * share].astype(BF16)


def down_terms(order, h, ho, w):
    rows = h.shape[0]
    hidden, feat = w.shape
    whole = pl.BlockSpec(memory_space=pltpu.VMEM)
    return pl.pallas_call(
        contract_hidden,
        in_specs=[pl.BlockSpec(memory_space=pltpu.SMEM), whole, whole, whole],
        out_specs=whole,
        out_shape=jax.ShapeDtypeStruct((rows, feat), BF16),
        cost_estimate=pl.CostEstimate(
            flops=2 * rows * hidden * feat, transcendentals=0, bytes_accessed=2 * hidden * feat + 4 * rows * hidden
        ),
        compiler_params=pltpu.CompilerParams(vmem_limit_bytes=40 << 20),
        name="down_terms",
    )(order, h, ho, w)


def after(value, *others):
    return lax.optimization_barrier((value,) + others)[0]


def as_rows(v, feat):
    row = jnp.concatenate(split3(v), axis=-1)
    return jnp.pad(row[..., None, :], [(0, 0)] * (v.ndim - 1) + [(0, 7), (0, feat - row.shape[-1])])


def from_row(row, n):
    hi, mid, lo = (row[..., k * n : (k + 1) * n].astype(F32) for k in range(3))
    return hi + mid + lo


def body(queries, keys, values, residual, norm_gain, routes, route_weight, w_gate, w_up, w_down):
    feat = residual.shape[1]
    half = w_gate.shape[0] // 2
    core = lax.axis_index("c")
    me = lax.axis_index("yl")
    order = jnp.stack([me, core]).astype(jnp.int32)

    def halves(which):
        cut = partial(lax.dynamic_slice_in_dim, start_index=which * half, slice_size=half, axis=0)
        return jnp.concatenate([cut(w_gate), cut(w_up)], axis=0)

    w_in = halves(core)
    w_in_other = swap(halves(1 - core), "c")

    chosen = routes[:, 0]
    expert_ids = jnp.arange(EXPERTS, dtype=jnp.int32)
    onehot = (chosen[:, None] == expert_ids[None, :]).astype(jnp.int32)
    slot_index = jnp.sum((jnp.cumsum(onehot, axis=0) - 1) * onehot, axis=1)
    slot_ids = jnp.arange(CAP, dtype=jnp.int32)
    taken = (chosen[None, None, :] == expert_ids[:, None, None]) & (
        slot_index[None, None, :] == slot_ids[None, :, None]
    )
    select = taken.astype(BF16)

    attn, (w_in, w_in_other) = attend(queries, keys, values, (w_in, w_in_other))
    mixed = residual.astype(F32) + attn.astype(F32)
    squares = jnp.sum(mixed * mixed, axis=1)
    packed = jnp.einsum(
        "ect,td->ecd", select, (mixed * norm_gain[None, :]).astype(BF16), preferred_element_type=F32
    ).astype(BF16)

    nz = lax.axis_size("z")
    sources = EXPERTS * lax.axis_size("xl")
    n = CAP // 2
    block = sources * n

    def all_to_all(x, axes):
        return lax.all_to_all(x, axes, split_axis=0, concat_axis=0, tiled=True)

    def along_z(x):
        return all_to_all(jnp.broadcast_to(x[None], (nz,) + x.shape), "z").reshape((nz,) + x.shape)

    squares = jnp.sum(jnp.where(taken, squares[None, None, :], 0.0), axis=2)
    rows = jnp.concatenate([packed, as_rows(squares, feat)], axis=1)
    rows = jnp.broadcast_to(rows[:, None], (EXPERTS, 2) + rows.shape[1:]).reshape(sources, CAP + 8, feat)
    rows = all_to_all(rows, GROUP)
    part_a, part_b = (rows[:, k * n : (k + 1) * n].reshape(block, feat) for k in range(2))
    x_a = along_z(part_a)
    squares = from_row(rows[:, CAP], CAP).reshape(sources, 2, n).transpose(1, 0, 2).reshape(2 * block)
    inverse = lax.rsqrt(lax.psum(squares, EXP) / D + 1e-05)
    x_a, inverse = lax.optimization_barrier((x_a, inverse))
    x_b = along_z(jnp.concatenate([part_b, as_rows(inverse, feat)], axis=0))

    def neighbour(x):
        return lax.ppermute(x, "yl", Y_XOR[1])

    def across(x):
        return lax.ppermute(x, "yl", Y_XOR[2])

    def pair_of(terms, got):
        return (terms[1].astype(F32) + got[got.shape[0] // 2 :].astype(F32)).astype(BF16)

    def hidden_of(terms, got, last, inverse):
        inverse = lax.dynamic_index_in_dim(inverse.reshape(4, -1), me, 0, keepdims=False)
        full = terms[0].astype(F32) + got[: got.shape[0] // 2].astype(F32) + last.astype(F32)
        full = full * inverse[:, None]
        return (jax.nn.silu(full[:, :half]) * full[:, half:]).astype(BF16)

    def down_of(two, other_two):
        hid = jnp.concatenate([two, other_two], axis=0)
        return down_terms(order, hid, swap(hid, "c"), w_down)

    def give_back(down):
        return all_to_all(down.reshape(nz, block, feat), "z")

    def over_z(back):
        return jnp.sum(back.astype(F32), axis=0).astype(BF16).reshape(sources, n, feat)

    terms_a = gate_up_terms(order, x_a, swap(x_a, "c"), w_in, w_in_other, block)
    got_a = neighbour(terms_a[2])
    x_b = after(x_b, got_a)
    inverse = from_row(x_b[:, block], 2 * block)
    last_a = across(pair_of(terms_a, got_a))
    terms_b = gate_up_terms(order, x_b, swap(x_b, "c"), w_in, w_in_other, block)
    last_a = after(last_a, *terms_b)
    hidden_a = hidden_of(terms_a, got_a, last_a, inverse[:, :block])
    got_b = neighbour(terms_b[2])
    two_a = jnp.concatenate([hidden_a, after(across(hidden_a), got_b)], axis=0)
    last_b = across(pair_of(terms_b, got_b))
    down_a = down_of(two_a, after(neighbour(two_a), last_b))
    back_a = give_back(down_a)
    hidden_b = hidden_of(terms_b, got_b, last_b, inverse[:, block:])
    two_b = jnp.concatenate([hidden_b, after(across(hidden_b), down_a)], axis=0)
    other_two_b = neighbour(two_b)
    back_a = after(back_a, other_two_b)
    back_b = give_back(down_of(two_b, other_two_b))
    returned = all_to_all(jnp.concatenate([over_z(back_a), over_z(back_b)], axis=1), GROUP)
    returned = jnp.sum(returned.reshape(EXPERTS, 2, CAP, feat).astype(F32), axis=1)
    moe_rows = jnp.einsum(
        "ect,ecd->td", taken.astype(F32), returned, precision=lax.Precision.HIGHEST, preferred_element_type=F32
    )
    return (route_weight[:, None] * moe_rows).astype(BF16)


def solution(mesh):
    fine = Mesh(mesh.devices.reshape(2, 2, 2, 8, 4, 2), CTX + EXP)
    wide = P(CTX, EXP)
    in_specs = (wide, wide, wide, wide, P(EXP), P(CTX, None), P(CTX), wide, wide, wide)
    return jax.shard_map(body, mesh=fine, in_specs=in_specs, out_specs=wide, check_vma=False)
```

```python
import math
from functools import partial

import jax
import jax.numpy as jnp
from jax import lax
from jax.experimental import pallas as pl
from jax.experimental.pallas import tpu as pltpu
from jax.sharding import Mesh, PartitionSpec as P

D = 6144
HD = 128
EXPERTS = 4
CAP = 24
F32 = jnp.float32
BF16 = jnp.bfloat16

CTX = ("yh", "xh", "xl", "z")
EXP = ("yl", "c")
HALF = ("xh", "xl", "z")
GROUP = ("yh", "xh", "xl")
SWAP = [(0, 1), (1, 0)]
Y_XOR = [[(i, i ^ k) for i in range(4)] for k in range(4)]


def swap(x, axis):
    return lax.ppermute(x, axis, SWAP)


def split3(v):
    hi = lax.reduce_precision(v, 8, 7)
    mid = lax.reduce_precision(v - hi, 8, 7)
    lo = (v - hi) - mid
    return [p.astype(BF16) for p in (hi, mid, lo)]


def softmax_block(base_ref, own_ref, far_ref, kv_ref, out_ref, lse_ref, message_ref):
    rows = own_ref.shape[0]
    count = kv_ref.shape[0]
    heads = own_ref.shape[1] // HD
    scale = 1.0 / math.sqrt(HD)
    keys, values = kv_ref[:, :HD], kv_ref[:, HD:]
    limit = base_ref[0] + lax.broadcasted_iota(jnp.int32, (rows, count), 0)
    allowed = lax.broadcasted_iota(jnp.int32, (rows, count), 1) <= limit
    lane = lax.broadcasted_iota(jnp.int32, (rows, HD), 1)
    tail = jnp.zeros((rows, HD), F32)
    for h in range(heads):
        cols = slice(h * HD, (h + 1) * HD)
        for far, ref in ((False, own_ref), (True, far_ref)):
            dots = lax.dot_general(ref[:, cols], keys, (((1,), (1,)), ((), ())), preferred_element_type=F32)
            if not far:
                dots = jnp.where(allowed, dots, -1e30)
            top = jnp.max(dots, axis=1, keepdims=True)
            weights = jnp.exp2((dots - top) * (scale * math.log2(math.e)))
            total = jnp.sum(weights, axis=1, keepdims=True)
            acc = jnp.dot(weights.astype(BF16), values, preferred_element_type=F32)
            out = acc / total
            lse = top * scale + jnp.log(total)
            if far:
                message_ref[:, cols] = out.astype(BF16)
                hi = lse.astype(BF16).astype(F32)
                mid = (lse - hi).astype(BF16).astype(F32)
                for k, part in enumerate((hi, mid, lse - hi - mid)):
                    tail = jnp.where(lane == k * heads + h, part, tail)
            else:
                out_ref[:, cols] = out
                lse_ref[:, cols] = jnp.broadcast_to(lse, (rows, HD))
    message_ref[:, heads * HD :] = tail.astype(BF16)


def attend(queries, keys, values, early):
    rows, width = queries.shape
    heads = width // HD
    yh = lax.axis_index("yh")
    foreign = lax.ppermute(queries, "yh", [(1, 0)])
    kv = jnp.concatenate([keys, values], axis=1)
    members = lax.axis_size(HALF)
    kv = lax.all_to_all(
        jnp.broadcast_to(kv[None], (members,) + kv.shape), HALF, split_axis=0, concat_axis=0, tiled=True
    ).reshape(members * rows, 2 * HD)
    kv, *early = lax.optimization_barrier((kv,) + early)
    whole = pl.BlockSpec(memory_space=pltpu.VMEM)
    out, lse, message = pl.pallas_call(
        softmax_block,
        in_specs=[pl.BlockSpec(memory_space=pltpu.SMEM), whole, whole, whole],
        out_specs=[whole, whole, whole],
        out_shape=[
            jax.ShapeDtypeStruct((rows, width), F32),
            jax.ShapeDtypeStruct((rows, width), F32),
            jax.ShapeDtypeStruct((rows, width + HD), BF16),
        ],
        cost_estimate=pl.CostEstimate(
            flops=8 * rows * width * members * rows,
            transcendentals=2 * rows * heads * members * rows,
            bytes_accessed=4 * members * rows * HD + 16 * rows * width,
        ),
        compiler_params=pltpu.CompilerParams(vmem_limit_bytes=48 << 20),
        name="softmax_block",
    )((lax.axis_index(HALF) * rows).astype(jnp.int32).reshape(1), queries, foreign, kv)
    got = lax.ppermute(message, "yh", [(0, 1)])
    parts = got[:, width : width + 3 * heads].astype(F32)
    got_lse = parts[:, :heads] + parts[:, heads : 2 * heads] + parts[:, 2 * heads :]
    share = jnp.where(yh == 1, jax.nn.sigmoid(jnp.repeat(got_lse, HD, axis=1) - lse), 0.0)
    return (out * (1.0 - share) + got[:, :width].astype(F32) * share).astype(BF16), early


def expand(order_ref, x_ref, o_ref, w_ref, wo_ref, *rest):
    out_refs, acc_ref = rest[:4], rest[4]
    contract = (((1,), (1,)), ((), ()))
    x, o = (r[...].reshape(acc_ref.shape[0], r.shape[-1]) for r in (x_ref, o_ref))
    acc_ref[...] = lax.dot_general(x, w_ref[...], contract, preferred_element_type=F32) + lax.dot_general(
        o, wo_ref[...], contract, preferred_element_type=F32
    )
    share = out_refs[0].shape[0]
    for i, ref in enumerate(out_refs):
        at = pl.multiple_of((order_ref[0] ^ i) * share, share)
        ref[...] = acc_ref[pl.ds(at, share), :].astype(BF16)


def gate_up_terms(order, x, other, w, wo, block):
    hidden, feat = w.shape
    cols = hidden // 2
    rows = x.shape[0] * block
    share = rows // 4
    spec = pl.BlockSpec((x.shape[0], block, feat), lambda n, o: (0, 0, 0))
    weight = pl.BlockSpec((cols, feat), lambda n, o: (n, 0))
    out = pl.BlockSpec((share, cols), lambda n, o: (0, n))
    shape = pltpu.HBM((share, hidden), BF16)
    return pl.pallas_call(
        expand,
        grid_spec=pltpu.PrefetchScalarGridSpec(
            num_scalar_prefetch=1,
            grid=(2,),
            in_specs=[spec, spec, weight, weight],
            out_specs=[out] * 4,
            scratch_shapes=[pltpu.VMEM((rows, cols), F32)],
        ),
        out_shape=[shape] * 4,
        cost_estimate=pl.CostEstimate(
            flops=4 * rows * hidden * feat, transcendentals=0, bytes_accessed=4 * hidden * feat + 2 * rows * hidden
        ),
        compiler_params=pltpu.CompilerParams(vmem_limit_bytes=40 << 20),
        name="gate_up_terms",
    )(order, x, other, *(pltpu.with_memory_space_constraint(v, pltpu.HBM) for v in (w, wo)))


def contract_hidden(order_ref, h_ref, ho_ref, w_ref, out_ref):
    core = order_ref[1]
    half = w_ref.shape[0] // 2
    own = pl.multiple_of(core * half, half)
    other = pl.multiple_of((1 - core) * half, half)
    acc = jnp.dot(h_ref[...], w_ref[pl.ds(own, half), :], preferred_element_type=F32)
    acc += jnp.dot(ho_ref[...], w_ref[pl.ds(other, half), :], preferred_element_type=F32)
    share = h_ref.shape[0] // 4
    for i in range(4):
        at = pl.multiple_of((order_ref[0] ^ i) * share, share)
        out_ref[pl.ds(at, share), :] = acc[i * share : (i + 1) * share].astype(BF16)


def down_terms(order, h, ho, w):
    rows = h.shape[0]
    hidden, feat = w.shape
    whole = pl.BlockSpec(memory_space=pltpu.VMEM)
    return pl.pallas_call(
        contract_hidden,
        in_specs=[pl.BlockSpec(memory_space=pltpu.SMEM), whole, whole, whole],
        out_specs=whole,
        out_shape=jax.ShapeDtypeStruct((rows, feat), BF16),
        cost_estimate=pl.CostEstimate(
            flops=2 * rows * hidden * feat, transcendentals=0, bytes_accessed=2 * hidden * feat + 4 * rows * hidden
        ),
        compiler_params=pltpu.CompilerParams(vmem_limit_bytes=40 << 20),
        name="down_terms",
    )(order, h, ho, w)


def after(value, *others):
    return lax.optimization_barrier((value,) + others)[0]


def as_rows(v, feat):
    row = jnp.concatenate(split3(v), axis=-1)
    return jnp.pad(row[..., None, :], [(0, 0)] * (v.ndim - 1) + [(0, 7), (0, feat - row.shape[-1])])


def from_row(row, n):
    hi, mid, lo = (row[..., k * n : (k + 1) * n].astype(F32) for k in range(3))
    return hi + mid + lo


def body(queries, keys, values, residual, norm_gain, routes, route_weight, w_gate, w_up, w_down):
    feat = residual.shape[1]
    half = w_gate.shape[0] // 2
    core = lax.axis_index("c")
    me = lax.axis_index("yl")
    order = jnp.stack([me, core]).astype(jnp.int32)

    def halves(which):
        cut = partial(lax.dynamic_slice_in_dim, start_index=which * half, slice_size=half, axis=0)
        return jnp.concatenate([cut(w_gate), cut(w_up)], axis=0)

    w_in = halves(core)
    w_in_other = swap(halves(1 - core), "c")

    chosen = routes[:, 0]
    expert_ids = jnp.arange(EXPERTS, dtype=jnp.int32)
    onehot = (chosen[:, None] == expert_ids[None, :]).astype(jnp.int32)
    slot_index = jnp.sum((jnp.cumsum(onehot, axis=0) - 1) * onehot, axis=1)
    slot_ids = jnp.arange(CAP, dtype=jnp.int32)
    taken = (chosen[None, None, :] == expert_ids[:, None, None]) & (
        slot_index[None, None, :] == slot_ids[None, :, None]
    )
    select = taken.astype(BF16)

    attn, (w_in, w_in_other) = attend(queries, keys, values, (w_in, w_in_other))
    mixed = residual.astype(F32) + attn.astype(F32)
    squares = jnp.sum(mixed * mixed, axis=1)
    packed = jnp.einsum(
        "ect,td->ecd", select, (mixed * norm_gain[None, :]).astype(BF16), preferred_element_type=F32
    ).astype(BF16)

    nz = lax.axis_size("z")
    sources = EXPERTS * lax.axis_size("xl")
    n = CAP // 2
    block = sources * n

    def all_to_all(x, axes):
        return lax.all_to_all(x, axes, split_axis=0, concat_axis=0, tiled=True)

    def along_z(x):
        return all_to_all(jnp.broadcast_to(x[None], (nz,) + x.shape), "z").reshape((nz,) + x.shape)

    squares = jnp.sum(jnp.where(taken, squares[None, None, :], 0.0), axis=2)
    rows = jnp.concatenate([packed, as_rows(squares, feat)], axis=1)
    rows = jnp.broadcast_to(rows[:, None], (EXPERTS, 2) + rows.shape[1:]).reshape(sources, CAP + 8, feat)
    rows = all_to_all(rows, GROUP)
    part_a, part_b = (rows[:, k * n : (k + 1) * n].reshape(block, feat) for k in range(2))
    x_a = along_z(part_a)
    squares = from_row(rows[:, CAP], CAP).reshape(sources, 2, n).transpose(1, 0, 2).reshape(2 * block)
    inverse = lax.rsqrt(lax.psum(squares, EXP) / D + 1e-05)
    x_a, inverse = lax.optimization_barrier((x_a, inverse))
    x_b = along_z(jnp.concatenate([part_b, as_rows(inverse, feat)], axis=0))

    def over_yl(parts):
        return [parts[0]] + [lax.ppermute(parts[i], "yl", Y_XOR[i]) for i in range(1, 4)]

    def hidden_of(parts, inverse):
        inverse = lax.dynamic_index_in_dim(inverse.reshape(4, -1), me, 0, keepdims=False)
        full = sum(p.astype(F32) for p in parts) * inverse[:, None]
        return (jax.nn.silu(full[:, :half]) * full[:, half:]).astype(BF16)

    def down_of(parts):
        hid = jnp.concatenate(parts, axis=0)
        return down_terms(order, hid, swap(hid, "c"), w_down)

    def give_back(down):
        return all_to_all(down.reshape(nz, block, feat), "z")

    def over_z(back):
        return jnp.sum(back.astype(F32), axis=0).astype(BF16).reshape(sources, n, feat)

    terms_a = gate_up_terms(order, x_a, swap(x_a, "c"), w_in, w_in_other, block)
    sums_a = over_yl(terms_a)
    x_b = after(x_b, *sums_a[2:])
    inverse = from_row(x_b[:, block], 2 * block)
    terms_b = gate_up_terms(order, x_b, swap(x_b, "c"), w_in, w_in_other, block)
    sums_a[1] = after(sums_a[1], *terms_b)
    hids_a = over_yl([hidden_of(sums_a, inverse[:, :block])] * 4)
    sums_b = over_yl(terms_b)
    hids_a[1] = after(hids_a[1], sums_b[3])
    down_a = down_of(hids_a)
    back_a = give_back(down_a)
    sums_b[1] = after(sums_b[1], down_a)
    hids_b = over_yl([hidden_of(sums_b, inverse[:, block:])] * 4)
    back_a = after(back_a, *hids_b[1:])
    back_b = give_back(down_of(hids_b))
    returned = all_to_all(jnp.concatenate([over_z(back_a), over_z(back_b)], axis=1), GROUP)
    returned = jnp.sum(returned.reshape(EXPERTS, 2, CAP, feat).astype(F32), axis=1)
    moe_rows = jnp.einsum(
        "ect,ecd->td", taken.astype(F32), returned, precision=lax.Precision.HIGHEST, preferred_element_type=F32
    )
    return (route_weight[:, None] * moe_rows).astype(BF16)


def solution(mesh):
    fine = Mesh(mesh.devices.reshape(2, 2, 2, 8, 4, 2), CTX + EXP)
    wide = P(CTX, EXP)
    in_specs = (wide, wide, wide, wide, P(EXP), P(CTX, None), P(CTX), wide, wide, wide)
    return jax.shard_map(body, mesh=fine, in_specs=in_specs, out_specs=wide, check_vma=False)
```

```python
import math
from functools import partial

import jax
import jax.numpy as jnp
from jax import lax
from jax.experimental import pallas as pl
from jax.experimental.pallas import tpu as pltpu
from jax.sharding import Mesh, PartitionSpec as P

D = 6144
HD = 128
EXPERTS = 4
CAP = 24
FIRST = 16
F32 = jnp.float32
BF16 = jnp.bfloat16

CTX = ("yh", "xh", "xl", "z")
EXP = ("yl", "c")
HALF = ("xh", "xl", "z")
GROUP = ("yh", "xh", "xl")
SWAP = [(0, 1), (1, 0)]
Y_XOR = [[(i, i ^ k) for i in range(4)] for k in range(4)]


def swap(x, axis):
    return lax.ppermute(x, axis, SWAP)


def split3(v):
    hi = lax.reduce_precision(v, 8, 7)
    mid = lax.reduce_precision(v - hi, 8, 7)
    lo = (v - hi) - mid
    return [p.astype(BF16) for p in (hi, mid, lo)]


def softmax_block(base_ref, own_ref, far_ref, kv_ref, out_ref, lse_ref, message_ref):
    rows = own_ref.shape[0]
    count = kv_ref.shape[0]
    heads = own_ref.shape[1] // HD
    scale = 1.0 / math.sqrt(HD)
    keys, values = kv_ref[:, :HD], kv_ref[:, HD:]
    limit = base_ref[0] + lax.broadcasted_iota(jnp.int32, (rows, count), 0)
    allowed = lax.broadcasted_iota(jnp.int32, (rows, count), 1) <= limit
    lane = lax.broadcasted_iota(jnp.int32, (rows, HD), 1)
    tail = jnp.zeros((rows, HD), F32)
    for h in range(heads):
        cols = slice(h * HD, (h + 1) * HD)
        for far, ref in ((False, own_ref), (True, far_ref)):
            dots = lax.dot_general(ref[:, cols], keys, (((1,), (1,)), ((), ())), preferred_element_type=F32)
            if not far:
                dots = jnp.where(allowed, dots, -1e30)
            top = jnp.max(dots, axis=1, keepdims=True)
            weights = jnp.exp2((dots - top) * (scale * math.log2(math.e)))
            total = jnp.sum(weights, axis=1, keepdims=True)
            acc = jnp.dot(weights.astype(BF16), values, preferred_element_type=F32)
            out = acc / total
            lse = top * scale + jnp.log(total)
            if far:
                message_ref[:, cols] = out.astype(BF16)
                hi = lse.astype(BF16).astype(F32)
                mid = (lse - hi).astype(BF16).astype(F32)
                for k, part in enumerate((hi, mid, lse - hi - mid)):
                    tail = jnp.where(lane == k * heads + h, part, tail)
            else:
                out_ref[:, cols] = out
                lse_ref[:, cols] = jnp.broadcast_to(lse, (rows, HD))
    message_ref[:, heads * HD :] = tail.astype(BF16)


def attend(queries, keys, values, early):
    rows, width = queries.shape
    heads = width // HD
    yh = lax.axis_index("yh")
    foreign = lax.ppermute(queries, "yh", [(1, 0)])
    kv = jnp.concatenate([keys, values], axis=1)
    members = lax.axis_size(HALF)
    kv = lax.all_to_all(
        jnp.broadcast_to(kv[None], (members,) + kv.shape), HALF, split_axis=0, concat_axis=0, tiled=True
    ).reshape(members * rows, 2 * HD)
    kv, *early = lax.optimization_barrier((kv,) + early)
    whole = pl.BlockSpec(memory_space=pltpu.VMEM)
    out, lse, message = pl.pallas_call(
        softmax_block,
        in_specs=[pl.BlockSpec(memory_space=pltpu.SMEM), whole, whole, whole],
        out_specs=[whole, whole, whole],
        out_shape=[
            jax.ShapeDtypeStruct((rows, width), F32),
            jax.ShapeDtypeStruct((rows, width), F32),
            jax.ShapeDtypeStruct((rows, width + HD), BF16),
        ],
        cost_estimate=pl.CostEstimate(
            flops=8 * rows * width * members * rows,
            transcendentals=2 * rows * heads * members * rows,
            bytes_accessed=4 * members * rows * HD + 16 * rows * width,
        ),
        compiler_params=pltpu.CompilerParams(vmem_limit_bytes=48 << 20),
        name="softmax_block",
    )((lax.axis_index(HALF) * rows).astype(jnp.int32).reshape(1), queries, foreign, kv)
    got = lax.ppermute(message, "yh", [(0, 1)])
    parts = got[:, width : width + 3 * heads].astype(F32)
    got_lse = parts[:, :heads] + parts[:, heads : 2 * heads] + parts[:, 2 * heads :]
    share = jnp.where(yh == 1, jax.nn.sigmoid(jnp.repeat(got_lse, HD, axis=1) - lse), 0.0)
    return (out * (1.0 - share) + got[:, :width].astype(F32) * share).astype(BF16), early


def expand(order_ref, x_ref, o_ref, w_ref, wo_ref, *rest):
    out_refs, acc_ref = rest[:4], rest[4]
    contract = (((1,), (1,)), ((), ()))
    x, o = (r[...].reshape(acc_ref.shape[0], r.shape[-1]) for r in (x_ref, o_ref))
    acc_ref[...] = lax.dot_general(x, w_ref[...], contract, preferred_element_type=F32) + lax.dot_general(
        o, wo_ref[...], contract, preferred_element_type=F32
    )
    share = out_refs[0].shape[0]
    for i, ref in enumerate(out_refs):
        at = pl.multiple_of((order_ref[0] ^ i) * share, share)
        ref[...] = acc_ref[pl.ds(at, share), :].astype(BF16)


def gate_up_terms(order, x, other, w, wo, block):
    hidden, feat = w.shape
    cols = hidden // 2
    rows = x.shape[0] * block
    share = rows // 4
    spec = pl.BlockSpec((x.shape[0], block, feat), lambda n, o: (0, 0, 0))
    weight = pl.BlockSpec((cols, feat), lambda n, o: (n, 0))
    out = pl.BlockSpec((share, cols), lambda n, o: (0, n))
    shape = pltpu.HBM((share, hidden), BF16)
    return pl.pallas_call(
        expand,
        grid_spec=pltpu.PrefetchScalarGridSpec(
            num_scalar_prefetch=1,
            grid=(2,),
            in_specs=[spec, spec, weight, weight],
            out_specs=[out] * 4,
            scratch_shapes=[pltpu.VMEM((rows, cols), F32)],
        ),
        out_shape=[shape] * 4,
        cost_estimate=pl.CostEstimate(
            flops=4 * rows * hidden * feat, transcendentals=0, bytes_accessed=4 * hidden * feat + 2 * rows * hidden
        ),
        compiler_params=pltpu.CompilerParams(vmem_limit_bytes=40 << 20),
        name="gate_up_terms",
    )(order, x, other, *(pltpu.with_memory_space_constraint(v, pltpu.HBM) for v in (w, wo)))


def contract_hidden(order_ref, h_ref, ho_ref, w_ref, out_ref):
    core = order_ref[1]
    half = w_ref.shape[0] // 2
    own = pl.multiple_of(core * half, half)
    other = pl.multiple_of((1 - core) * half, half)
    acc = jnp.dot(h_ref[...], w_ref[pl.ds(own, half), :], preferred_element_type=F32)
    acc += jnp.dot(ho_ref[...], w_ref[pl.ds(other, half), :], preferred_element_type=F32)
    share = h_ref.shape[0] // 4
    for i in range(4):
        at = pl.multiple_of((order_ref[0] ^ i) * share, share)
        out_ref[pl.ds(at, share), :] = acc[i * share : (i + 1) * share].astype(BF16)


def down_terms(order, h, ho, w):
    rows = h.shape[0]
    hidden, feat = w.shape
    whole = pl.BlockSpec(memory_space=pltpu.VMEM)
    return pl.pallas_call(
        contract_hidden,
        in_specs=[pl.BlockSpec(memory_space=pltpu.SMEM), whole, whole, whole],
        out_specs=whole,
        out_shape=jax.ShapeDtypeStruct((rows, feat), BF16),
        cost_estimate=pl.CostEstimate(
            flops=2 * rows * hidden * feat, transcendentals=0, bytes_accessed=2 * hidden * feat + 4 * rows * hidden
        ),
        compiler_params=pltpu.CompilerParams(vmem_limit_bytes=40 << 20),
        name="down_terms",
    )(order, h, ho, w)


def after(value, *others):
    return lax.optimization_barrier((value,) + others)[0]


def as_rows(v, feat):
    row = jnp.concatenate(split3(v), axis=-1)
    return jnp.pad(row[..., None, :], [(0, 0)] * (v.ndim - 1) + [(0, 7), (0, feat - row.shape[-1])])


def from_row(row, n):
    hi, mid, lo = (row[..., k * n : (k + 1) * n].astype(F32) for k in range(3))
    return hi + mid + lo


def body(queries, keys, values, residual, norm_gain, routes, route_weight, w_gate, w_up, w_down):
    feat = residual.shape[1]
    half = w_gate.shape[0] // 2
    core = lax.axis_index("c")
    me = lax.axis_index("yl")
    order = jnp.stack([me, core]).astype(jnp.int32)

    def halves(which):
        cut = partial(lax.dynamic_slice_in_dim, start_index=which * half, slice_size=half, axis=0)
        return jnp.concatenate([cut(w_gate), cut(w_up)], axis=0)

    w_in = halves(core)
    w_in_other = swap(halves(1 - core), "c")

    chosen = routes[:, 0]
    expert_ids = jnp.arange(EXPERTS, dtype=jnp.int32)
    onehot = (chosen[:, None] == expert_ids[None, :]).astype(jnp.int32)
    slot_index = jnp.sum((jnp.cumsum(onehot, axis=0) - 1) * onehot, axis=1)
    slot_ids = jnp.arange(CAP, dtype=jnp.int32)
    taken = (chosen[None, None, :] == expert_ids[:, None, None]) & (
        slot_index[None, None, :] == slot_ids[None, :, None]
    )
    select = taken.astype(BF16)

    attn, (w_in, w_in_other) = attend(queries, keys, values, (w_in, w_in_other))
    mixed = residual.astype(F32) + attn.astype(F32)
    squares = jnp.sum(mixed * mixed, axis=1)
    packed = jnp.einsum(
        "ect,td->ecd", select, (mixed * norm_gain[None, :]).astype(BF16), preferred_element_type=F32
    ).astype(BF16)

    nz = lax.axis_size("z")
    sources = EXPERTS * lax.axis_size("xl")
    block_a, block_b = sources * FIRST, sources * (CAP - FIRST)

    def all_to_all(x, axes):
        return lax.all_to_all(x, axes, split_axis=0, concat_axis=0, tiled=True)

    def along_z(x):
        return all_to_all(jnp.broadcast_to(x[None], (nz,) + x.shape), "z").reshape((nz,) + x.shape)

    squares = jnp.sum(jnp.where(taken, squares[None, None, :], 0.0), axis=2)
    rows = jnp.concatenate([packed, as_rows(squares, feat)], axis=1)
    rows = jnp.broadcast_to(rows[:, None], (EXPERTS, 2) + rows.shape[1:]).reshape(sources, CAP + 8, feat)
    rows = all_to_all(rows, GROUP)
    part_a, part_b = rows[:, :FIRST].reshape(block_a, feat), rows[:, FIRST:CAP].reshape(block_b, feat)
    x_a = along_z(part_a)
    squares = from_row(rows[:, CAP], CAP)
    squares = jnp.concatenate([squares[:, :FIRST].reshape(block_a), squares[:, FIRST:].reshape(block_b)])
    inverse = lax.rsqrt(lax.psum(squares, EXP) / D + 1e-05)
    x_a, inverse = lax.optimization_barrier((x_a, inverse))
    x_b = along_z(jnp.concatenate([part_b, as_rows(inverse, feat)], axis=0))

    def over_yl(parts):
        return [parts[0]] + [lax.ppermute(parts[i], "yl", Y_XOR[i]) for i in range(1, 4)]

    def hidden_of(parts, inverse):
        inverse = lax.dynamic_index_in_dim(inverse.reshape(4, -1), me, 0, keepdims=False)
        full = sum(p.astype(F32) for p in parts) * inverse[:, None]
        return (jax.nn.silu(full[:, :half]) * full[:, half:]).astype(BF16)

    def down_of(parts):
        hid = jnp.concatenate(parts, axis=0)
        return down_terms(order, hid, swap(hid, "c"), w_down)

    def give_back(down):
        return all_to_all(down.reshape(nz, -1, feat), "z")

    def over_z(back):
        return jnp.sum(back.astype(F32), axis=0).astype(BF16).reshape(sources, -1, feat)

    terms_a = gate_up_terms(order, x_a, swap(x_a, "c"), w_in, w_in_other, block_a)
    sums_a = over_yl(terms_a)
    x_b = after(x_b, sums_a[3])
    inverse = from_row(x_b[:, block_b], block_a + block_b)
    terms_b = gate_up_terms(order, x_b, swap(x_b, "c"), w_in, w_in_other, block_b)
    sums_a[1] = after(sums_a[1], *terms_b)
    hids_a = over_yl([hidden_of(sums_a, inverse[:, :block_a])] * 4)
    sums_b = over_yl(terms_b)
    hids_a[1] = after(hids_a[1], sums_b[3])
    down_a = down_of(hids_a)
    back_a = give_back(down_a)
    sums_b[1] = after(sums_b[1], down_a)
    hids_b = over_yl([hidden_of(sums_b, inverse[:, block_a:])] * 4)
    back_a = after(back_a, *hids_b[1:])
    back_b = give_back(after(down_of(hids_b), back_a))
    returned = all_to_all(jnp.concatenate([over_z(back_a), over_z(back_b)], axis=1), GROUP)
    returned = jnp.sum(returned.reshape(EXPERTS, 2, CAP, feat).astype(F32), axis=1)
    moe_rows = jnp.einsum(
        "ect,ecd->td", taken.astype(F32), returned, precision=lax.Precision.HIGHEST, preferred_element_type=F32
    )
    return (route_weight[:, None] * moe_rows).astype(BF16)


def solution(mesh):
    fine = Mesh(mesh.devices.reshape(2, 2, 2, 8, 4, 2), CTX + EXP)
    wide = P(CTX, EXP)
    in_specs = (wide, wide, wide, wide, P(EXP), P(CTX, None), P(CTX), wide, wide, wide)
    return jax.shard_map(body, mesh=fine, in_specs=in_specs, out_specs=wide, check_vma=False)
```

```python
import math
from functools import partial

import jax
import jax.numpy as jnp
from jax import lax
from jax.experimental import pallas as pl
from jax.experimental.pallas import tpu as pltpu
from jax.sharding import Mesh, PartitionSpec as P

D = 6144
HD = 128
EXPERTS = 4
CAP = 24
F32 = jnp.float32
BF16 = jnp.bfloat16

CTX = ("yh", "xh", "xl", "z")
EXP = ("yl", "c")
HALF = ("xh", "xl", "z")
GROUP = ("yh", "xh", "xl")
SWAP = [(0, 1), (1, 0)]
Y_XOR = [[(i, i ^ k) for i in range(4)] for k in range(4)]


def swap(x, axis):
    return lax.ppermute(x, axis, SWAP)


def split3(v):
    hi = lax.reduce_precision(v, 8, 7)
    mid = lax.reduce_precision(v - hi, 8, 7)
    lo = (v - hi) - mid
    return [p.astype(BF16) for p in (hi, mid, lo)]


def softmax_block(base_ref, own_ref, far_ref, kv_ref, out_ref, lse_ref, message_ref):
    rows = own_ref.shape[0]
    count = kv_ref.shape[0]
    heads = own_ref.shape[1] // HD
    scale = 1.0 / math.sqrt(HD)
    keys, values = kv_ref[:, :HD], kv_ref[:, HD:]
    row = lax.broadcasted_iota(jnp.int32, (2 * rows, count), 0)
    limit = jnp.where(row < rows, base_ref[0] + row, count)
    allowed = lax.broadcasted_iota(jnp.int32, (2 * rows, count), 1) <= limit
    lane = lax.broadcasted_iota(jnp.int32, (rows, HD), 1)
    tail = jnp.zeros((rows, HD), F32)
    for h in range(heads):
        cols = slice(h * HD, (h + 1) * HD)
        both = jnp.concatenate([own_ref[:, cols], far_ref[:, cols]], axis=0)
        dots = lax.dot_general(both, keys, (((1,), (1,)), ((), ())), preferred_element_type=F32)
        dots = jnp.where(allowed, dots, -1e30)
        top = jnp.max(dots, axis=1, keepdims=True)
        weights = jnp.exp2((dots - top) * (scale * math.log2(math.e)))
        total = jnp.sum(weights, axis=1, keepdims=True)
        out = jnp.dot(weights.astype(BF16), values, preferred_element_type=F32) / total
        lse = top * scale + jnp.log(total)
        out_ref[:, cols] = out[:rows]
        lse_ref[:, cols] = jnp.broadcast_to(lse[:rows], (rows, HD))
        message_ref[:, cols] = out[rows:].astype(BF16)
        lse = lse[rows:]
        hi = lse.astype(BF16).astype(F32)
        mid = (lse - hi).astype(BF16).astype(F32)
        for k, part in enumerate((hi, mid, lse - hi - mid)):
            tail = jnp.where(lane == k * heads + h, part, tail)
    message_ref[:, heads * HD :] = tail.astype(BF16)


def attend(queries, keys, values):
    rows, width = queries.shape
    heads = width // HD
    yh = lax.axis_index("yh")
    foreign = lax.ppermute(queries, "yh", [(1, 0)])
    kv = jnp.concatenate([keys, values], axis=1)
    members = lax.axis_size(HALF)
    for axes in ("z", ("xh", "xl")):
        copies = jnp.broadcast_to(kv[None], (lax.axis_size(axes),) + kv.shape)
        kv = lax.all_to_all(copies, axes, split_axis=0, concat_axis=0, tiled=True).reshape(-1, 2 * HD)
    whole = pl.BlockSpec(memory_space=pltpu.VMEM)
    out, lse, message = pl.pallas_call(
        softmax_block,
        in_specs=[pl.BlockSpec(memory_space=pltpu.SMEM), whole, whole, whole],
        out_specs=[whole, whole, whole],
        out_shape=[
            jax.ShapeDtypeStruct((rows, width), F32),
            jax.ShapeDtypeStruct((rows, width), F32),
            jax.ShapeDtypeStruct((rows, width + HD), BF16),
        ],
        cost_estimate=pl.CostEstimate(
            flops=8 * rows * width * members * rows,
            transcendentals=2 * rows * heads * members * rows,
            bytes_accessed=4 * members * rows * HD + 16 * rows * width,
        ),
        compiler_params=pltpu.CompilerParams(vmem_limit_bytes=48 << 20),
        name="softmax_block",
    )((lax.axis_index(HALF) * rows).astype(jnp.int32).reshape(1), queries, foreign, kv)
    got = lax.ppermute(message, "yh", [(0, 1)])
    parts = got[:, width : width + 3 * heads].astype(F32)
    got_lse = parts[:, :heads] + parts[:, heads : 2 * heads] + parts[:, 2 * heads :]
    share = jnp.where(yh == 1, jax.nn.sigmoid(jnp.repeat(got_lse, HD, axis=1) - lse), 0.0)
    return (out * (1.0 - share) + got[:, :width].astype(F32) * share).astype(BF16)


def expand(order_ref, x_ref, o_ref, w_ref, wo_ref, *rest):
    out_refs, acc_ref = rest[:4], rest[4]
    contract = (((1,), (1,)), ((), ()))
    x, o = (r[...].reshape(acc_ref.shape[0], r.shape[-1]) for r in (x_ref, o_ref))
    acc_ref[...] = lax.dot_general(x, w_ref[...], contract, preferred_element_type=F32) + lax.dot_general(
        o, wo_ref[...], contract, preferred_element_type=F32
    )
    share = out_refs[0].shape[0]
    for i, ref in enumerate(out_refs):
        at = pl.multiple_of((order_ref[0] ^ i) * share, share)
        ref[...] = acc_ref[pl.ds(at, share), :].astype(BF16)


def gate_up_terms(order, x, other, w, wo, block):
    hidden, feat = w.shape
    cols = hidden // 2
    rows = x.shape[0] * block
    share = rows // 4
    spec = pl.BlockSpec((x.shape[0], block, feat), lambda n, o: (0, 0, 0))
    weight = pl.BlockSpec((cols, feat), lambda n, o: (n, 0))
    out = pl.BlockSpec((share, cols), lambda n, o: (0, n))
    shape = pltpu.HBM((share, hidden), BF16)
    return pl.pallas_call(
        expand,
        grid_spec=pltpu.PrefetchScalarGridSpec(
            num_scalar_prefetch=1,
            grid=(2,),
            in_specs=[spec, spec, weight, weight],
            out_specs=[out] * 4,
            scratch_shapes=[pltpu.VMEM((rows, cols), F32)],
        ),
        out_shape=[shape] * 4,
        cost_estimate=pl.CostEstimate(
            flops=4 * rows * hidden * feat, transcendentals=0, bytes_accessed=4 * hidden * feat + 2 * rows * hidden
        ),
        compiler_params=pltpu.CompilerParams(vmem_limit_bytes=40 << 20),
        name="gate_up_terms",
    )(order, x, other, *(pltpu.with_memory_space_constraint(v, pltpu.HBM) for v in (w, wo)))


def contract_hidden(order_ref, h_ref, ho_ref, w_ref, out_ref):
    core = order_ref[1]
    half = w_ref.shape[0] // 2
    own = pl.multiple_of(core * half, half)
    other = pl.multiple_of((1 - core) * half, half)
    acc = jnp.dot(h_ref[...], w_ref[pl.ds(own, half), :], preferred_element_type=F32)
    acc += jnp.dot(ho_ref[...], w_ref[pl.ds(other, half), :], preferred_element_type=F32)
    share = h_ref.shape[0] // 4
    for i in range(4):
        at = pl.multiple_of((order_ref[0] ^ i) * share, share)
        out_ref[pl.ds(at, share), :] = acc[i * share : (i + 1) * share].astype(BF16)


def down_terms(order, h, ho, w):
    rows = h.shape[0]
    hidden, feat = w.shape
    whole = pl.BlockSpec(memory_space=pltpu.VMEM)
    return pl.pallas_call(
        contract_hidden,
        in_specs=[pl.BlockSpec(memory_space=pltpu.SMEM), whole, whole, whole],
        out_specs=whole,
        out_shape=jax.ShapeDtypeStruct((rows, feat), BF16),
        cost_estimate=pl.CostEstimate(
            flops=2 * rows * hidden * feat, transcendentals=0, bytes_accessed=2 * hidden * feat + 4 * rows * hidden
        ),
        compiler_params=pltpu.CompilerParams(vmem_limit_bytes=40 << 20),
        name="down_terms",
    )(order, h, ho, w)


def after(value, *others):
    return lax.optimization_barrier((value,) + others)[0]


def as_rows(v, feat):
    row = jnp.concatenate(split3(v), axis=-1)
    return jnp.pad(row[..., None, :], [(0, 0)] * (v.ndim - 1) + [(0, 7), (0, feat - row.shape[-1])])


def from_row(row, n):
    hi, mid, lo = (row[..., k * n : (k + 1) * n].astype(F32) for k in range(3))
    return hi + mid + lo


def body(queries, keys, values, residual, norm_gain, routes, route_weight, w_gate, w_up, w_down):
    feat = residual.shape[1]
    half = w_gate.shape[0] // 2
    core = lax.axis_index("c")
    me = lax.axis_index("yl")
    order = jnp.stack([me, core]).astype(jnp.int32)

    def prepare(*weights):
        def halves(which):
            cut = partial(lax.dynamic_slice_in_dim, start_index=which * half, slice_size=half, axis=0)
            return jnp.concatenate([cut(w) for w in weights], axis=0)

        return halves(core), swap(halves(1 - core), "c")

    chosen = routes[:, 0]
    expert_ids = jnp.arange(EXPERTS, dtype=jnp.int32)
    onehot = (chosen[:, None] == expert_ids[None, :]).astype(jnp.int32)
    slot_index = jnp.sum((jnp.cumsum(onehot, axis=0) - 1) * onehot, axis=1)
    slot_ids = jnp.arange(CAP, dtype=jnp.int32)
    taken = (chosen[None, None, :] == expert_ids[:, None, None]) & (
        slot_index[None, None, :] == slot_ids[None, :, None]
    )
    select = taken.astype(BF16)

    attn = attend(queries, keys, values)
    mixed = residual.astype(F32) + attn.astype(F32)
    squares = jnp.sum(mixed * mixed, axis=1)
    packed = jnp.einsum(
        "ect,td->ecd", select, (mixed * norm_gain[None, :]).astype(BF16), preferred_element_type=F32
    ).astype(BF16)

    nz = lax.axis_size("z")
    sources = EXPERTS * lax.axis_size("xl")
    n = CAP // 2
    block = sources * n

    def all_to_all(x, axes):
        return lax.all_to_all(x, axes, split_axis=0, concat_axis=0, tiled=True)

    def along_z(x):
        return all_to_all(jnp.broadcast_to(x[None], (nz,) + x.shape), "z").reshape((nz,) + x.shape)

    squares = jnp.sum(jnp.where(taken, squares[None, None, :], 0.0), axis=2)
    rows = jnp.concatenate([packed, as_rows(squares, feat)], axis=1)
    rows = jnp.broadcast_to(rows[:, None], (EXPERTS, 2) + rows.shape[1:]).reshape(sources, CAP + 8, feat)
    rows = all_to_all(rows, GROUP)
    part_a, part_b = (rows[:, k * n : (k + 1) * n].reshape(block, feat) for k in range(2))
    x_a = along_z(part_a)
    squares = from_row(rows[:, CAP], CAP).reshape(sources, 2, n).transpose(1, 0, 2).reshape(2 * block)
    inverse = lax.rsqrt(lax.psum(squares, EXP) / D + 1e-05)
    inverse, w_gate, w_up = lax.optimization_barrier((inverse, w_gate, w_up))
    x_a, w_in, w_in_other = lax.optimization_barrier((x_a,) + prepare(w_gate, w_up))
    x_b = along_z(jnp.concatenate([part_b, as_rows(inverse, feat)], axis=0))

    def over_yl(parts):
        return [parts[0]] + [lax.ppermute(parts[i], "yl", Y_XOR[i]) for i in range(1, 4)]

    def hidden_of(parts, inverse):
        inverse = lax.dynamic_index_in_dim(inverse.reshape(4, -1), me, 0, keepdims=False)
        full = sum(p.astype(F32) for p in parts) * inverse[:, None]
        return (jax.nn.silu(full[:, :half]) * full[:, half:]).astype(BF16)

    def down_of(parts):
        hid = jnp.concatenate(parts, axis=0)
        return down_terms(order, hid, swap(hid, "c"), w_down)

    def give_back(down):
        return all_to_all(down.reshape(nz, block, feat), "z")

    def over_z(back):
        return jnp.sum(back.astype(F32), axis=0).astype(BF16).reshape(sources, n, feat)

    terms_a = gate_up_terms(order, x_a, swap(x_a, "c"), w_in, w_in_other, block)
    sums_a = over_yl(terms_a)
    x_b = after(x_b, sums_a[3])
    inverse = from_row(x_b[:, block], 2 * block)
    terms_b = gate_up_terms(order, x_b, swap(x_b, "c"), w_in, w_in_other, block)
    sums_a[1] = after(sums_a[1], *terms_b)
    hids_a = over_yl([hidden_of(sums_a, inverse[:, :block])] * 4)
    sums_b = over_yl(terms_b)
    hids_a[1] = after(hids_a[1], sums_b[3])
    down_a = down_of(hids_a)
    back_a = give_back(down_a)
    sums_b[1] = after(sums_b[1], down_a)
    hids_b = over_yl([hidden_of(sums_b, inverse[:, block:])] * 4)
    back_a = after(back_a, *hids_b[1:])
    back_b = give_back(down_of(hids_b))
    returned = all_to_all(jnp.concatenate([over_z(back_a), over_z(back_b)], axis=1), GROUP)
    returned = jnp.sum(returned.reshape(EXPERTS, 2, CAP, feat).astype(F32), axis=1)
    moe_rows = jnp.einsum(
        "ect,ecd->td", taken.astype(F32), returned, precision=lax.Precision.HIGHEST, preferred_element_type=F32
    )
    return (route_weight[:, None] * moe_rows).astype(BF16)


def solution(mesh):
    fine = Mesh(mesh.devices.reshape(2, 2, 2, 8, 4, 2), CTX + EXP)
    wide = P(CTX, EXP)
    in_specs = (wide, wide, wide, wide, P(EXP), P(CTX, None), P(CTX), wide, wide, wide)
    return jax.shard_map(body, mesh=fine, in_specs=in_specs, out_specs=wide, check_vma=False)
```

```python
import math
from functools import partial

import jax
import jax.numpy as jnp
from jax import lax
from jax.experimental import pallas as pl
from jax.experimental.pallas import tpu as pltpu
from jax.sharding import Mesh, PartitionSpec as P

D = 6144
HD = 128
EXPERTS = 4
CAP = 24
F32 = jnp.float32
BF16 = jnp.bfloat16

CTX = ("yh", "xh", "xl", "z")
EXP = ("yl", "c")
HALF = ("xh", "xl", "z")
GROUP = ("yh", "xh", "xl")
SWAP = [(0, 1), (1, 0)]
Y_XOR = [[(i, i ^ k) for i in range(4)] for k in range(4)]


def swap(x, axis):
    return lax.ppermute(x, axis, SWAP)


def split3(v):
    hi = lax.reduce_precision(v, 8, 7)
    mid = lax.reduce_precision(v - hi, 8, 7)
    lo = (v - hi) - mid
    return [p.astype(BF16) for p in (hi, mid, lo)]


def softmax_block(base_ref, own_ref, far_ref, kv_ref, out_ref, lse_ref, message_ref):
    rows = own_ref.shape[0]
    count = kv_ref.shape[0]
    heads = own_ref.shape[1] // HD
    scale = 1.0 / math.sqrt(HD)
    keys, values = kv_ref[:, :HD], kv_ref[:, HD:]
    row = lax.broadcasted_iota(jnp.int32, (2 * rows, count), 0)
    limit = jnp.where(row < rows, base_ref[0] + row, count)
    allowed = lax.broadcasted_iota(jnp.int32, (2 * rows, count), 1) <= limit
    lane = lax.broadcasted_iota(jnp.int32, (rows, HD), 1)
    tail = jnp.zeros((rows, HD), F32)
    for h in range(heads):
        cols = slice(h * HD, (h + 1) * HD)
        both = jnp.concatenate([own_ref[:, cols], far_ref[:, cols]], axis=0)
        dots = lax.dot_general(both, keys, (((1,), (1,)), ((), ())), preferred_element_type=F32)
        dots = jnp.where(allowed, dots, -1e30)
        top = jnp.max(dots, axis=1, keepdims=True)
        weights = jnp.exp2((dots - top) * (scale * math.log2(math.e)))
        total = jnp.sum(weights, axis=1, keepdims=True)
        out = jnp.dot(weights.astype(BF16), values, preferred_element_type=F32) / total
        lse = top * scale + jnp.log(total)
        out_ref[:, cols] = out[:rows]
        lse_ref[:, cols] = jnp.broadcast_to(lse[:rows], (rows, HD))
        message_ref[:, cols] = out[rows:].astype(BF16)
        lse = lse[rows:]
        hi = lse.astype(BF16).astype(F32)
        mid = (lse - hi).astype(BF16).astype(F32)
        for k, part in enumerate((hi, mid, lse - hi - mid)):
            tail = jnp.where(lane == k * heads + h, part, tail)
    message_ref[:, heads * HD :] = tail.astype(BF16)


def attend(queries, keys, values):
    rows, width = queries.shape
    heads = width // HD
    yh = lax.axis_index("yh")
    foreign = lax.ppermute(queries, "yh", [(1, 0)])
    kv = jnp.concatenate([keys, values], axis=1)
    members = lax.axis_size(HALF)
    for axes in ("z", ("xh", "xl")):
        copies = jnp.broadcast_to(kv[None], (lax.axis_size(axes),) + kv.shape)
        kv = lax.all_to_all(copies, axes, split_axis=0, concat_axis=0, tiled=True).reshape(-1, 2 * HD)
    whole = pl.BlockSpec(memory_space=pltpu.VMEM)
    out, lse, message = pl.pallas_call(
        softmax_block,
        in_specs=[pl.BlockSpec(memory_space=pltpu.SMEM), whole, whole, whole],
        out_specs=[whole, whole, whole],
        out_shape=[
            jax.ShapeDtypeStruct((rows, width), F32),
            jax.ShapeDtypeStruct((rows, width), F32),
            jax.ShapeDtypeStruct((rows, width + HD), BF16),
        ],
        cost_estimate=pl.CostEstimate(
            flops=8 * rows * width * members * rows,
            transcendentals=2 * rows * heads * members * rows,
            bytes_accessed=4 * members * rows * HD + 16 * rows * width,
        ),
        compiler_params=pltpu.CompilerParams(vmem_limit_bytes=48 << 20),
        name="softmax_block",
    )((lax.axis_index(HALF) * rows).astype(jnp.int32).reshape(1), queries, foreign, kv)
    got = lax.ppermute(message, "yh", [(0, 1)])
    parts = got[:, width : width + 3 * heads].astype(F32)
    got_lse = parts[:, :heads] + parts[:, heads : 2 * heads] + parts[:, 2 * heads :]
    share = jnp.where(yh == 1, jax.nn.sigmoid(jnp.repeat(got_lse, HD, axis=1) - lse), 0.0)
    return (out * (1.0 - share) + got[:, :width].astype(F32) * share).astype(BF16)


def expand(order_ref, x_ref, o_ref, w_ref, wo_ref, *rest):
    out_refs, acc_ref = rest[:4], rest[4]
    contract = (((1,), (1,)), ((), ()))
    x, o = (r[...].reshape(acc_ref.shape[0], r.shape[-1]) for r in (x_ref, o_ref))
    acc_ref[...] = lax.dot_general(x, w_ref[...], contract, preferred_element_type=F32) + lax.dot_general(
        o, wo_ref[...], contract, preferred_element_type=F32
    )
    share = out_refs[0].shape[0]
    for i, ref in enumerate(out_refs):
        at = pl.multiple_of((order_ref[0] ^ i) * share, share)
        ref[...] = acc_ref[pl.ds(at, share), :].astype(BF16)


def gate_up_terms(order, x, other, w, wo, block):
    hidden, feat = w.shape
    cols = hidden // 2
    rows = x.shape[0] * block
    share = rows // 4
    spec = pl.BlockSpec((x.shape[0], block, feat), lambda n, o: (0, 0, 0))
    weight = pl.BlockSpec((cols, feat), lambda n, o: (n, 0))
    out = pl.BlockSpec((share, cols), lambda n, o: (0, n))
    shape = pltpu.HBM((share, hidden), BF16)
    return pl.pallas_call(
        expand,
        grid_spec=pltpu.PrefetchScalarGridSpec(
            num_scalar_prefetch=1,
            grid=(2,),
            in_specs=[spec, spec, weight, weight],
            out_specs=[out] * 4,
            scratch_shapes=[pltpu.VMEM((rows, cols), F32)],
        ),
        out_shape=[shape] * 4,
        cost_estimate=pl.CostEstimate(
            flops=4 * rows * hidden * feat, transcendentals=0, bytes_accessed=4 * hidden * feat + 2 * rows * hidden
        ),
        compiler_params=pltpu.CompilerParams(vmem_limit_bytes=40 << 20),
        name="gate_up_terms",
    )(order, x, other, *(pltpu.with_memory_space_constraint(v, pltpu.HBM) for v in (w, wo)))


def contract_hidden(order_ref, h_ref, ho_ref, w_ref, out_ref):
    core = order_ref[1]
    half = w_ref.shape[0] // 2
    own = pl.multiple_of(core * half, half)
    other = pl.multiple_of((1 - core) * half, half)
    acc = jnp.dot(h_ref[...], w_ref[pl.ds(own, half), :], preferred_element_type=F32)
    acc += jnp.dot(ho_ref[...], w_ref[pl.ds(other, half), :], preferred_element_type=F32)
    share = h_ref.shape[0] // 4
    for i in range(4):
        at = pl.multiple_of((order_ref[0] ^ i) * share, share)
        out_ref[pl.ds(at, share), :] = acc[i * share : (i + 1) * share].astype(BF16)


def down_terms(order, h, ho, w):
    rows = h.shape[0]
    hidden, feat = w.shape
    whole = pl.BlockSpec(memory_space=pltpu.VMEM)
    return pl.pallas_call(
        contract_hidden,
        in_specs=[pl.BlockSpec(memory_space=pltpu.SMEM), whole, whole, whole],
        out_specs=whole,
        out_shape=jax.ShapeDtypeStruct((rows, feat), BF16),
        cost_estimate=pl.CostEstimate(
            flops=2 * rows * hidden * feat, transcendentals=0, bytes_accessed=2 * hidden * feat + 4 * rows * hidden
        ),
        compiler_params=pltpu.CompilerParams(vmem_limit_bytes=40 << 20),
        name="down_terms",
    )(order, h, ho, w)


def after(value, *others):
    return lax.optimization_barrier((value,) + others)[0]


def as_rows(v, feat):
    row = jnp.concatenate(split3(v), axis=-1)
    return jnp.pad(row[..., None, :], [(0, 0)] * (v.ndim - 1) + [(0, 7), (0, feat - row.shape[-1])])


def from_row(row, n):
    hi, mid, lo = (row[..., k * n : (k + 1) * n].astype(F32) for k in range(3))
    return hi + mid + lo


def body(queries, keys, values, residual, norm_gain, routes, route_weight, w_gate, w_up, w_down):
    feat = residual.shape[1]
    half = w_gate.shape[0] // 2
    core = lax.axis_index("c")
    me = lax.axis_index("yl")
    order = jnp.stack([me, core]).astype(jnp.int32)

    def prepare(*weights):
        def halves(which):
            cut = partial(lax.dynamic_slice_in_dim, start_index=which * half, slice_size=half, axis=0)
            return jnp.concatenate([cut(w) for w in weights], axis=0)

        return halves(core), swap(halves(1 - core), "c")

    chosen = routes[:, 0]
    expert_ids = jnp.arange(EXPERTS, dtype=jnp.int32)
    onehot = (chosen[:, None] == expert_ids[None, :]).astype(jnp.int32)
    slot_index = jnp.sum((jnp.cumsum(onehot, axis=0) - 1) * onehot, axis=1)
    slot_ids = jnp.arange(CAP, dtype=jnp.int32)
    taken = (chosen[None, None, :] == expert_ids[:, None, None]) & (
        slot_index[None, None, :] == slot_ids[None, :, None]
    )
    select = taken.astype(BF16)

    attn = attend(queries, keys, values)
    mixed = residual.astype(F32) + attn.astype(F32)
    squares = jnp.sum(mixed * mixed, axis=1)
    packed = jnp.einsum(
        "ect,td->ecd", select, (mixed * norm_gain[None, :]).astype(BF16), preferred_element_type=F32
    ).astype(BF16)

    nz = lax.axis_size("z")
    sources = EXPERTS * lax.axis_size("xl")
    n = CAP // 2
    block = sources * n

    def all_to_all(x, axes):
        return lax.all_to_all(x, axes, split_axis=0, concat_axis=0, tiled=True)

    def along_z(x):
        return all_to_all(jnp.broadcast_to(x[None], (nz,) + x.shape), "z").reshape((nz,) + x.shape)

    squares = jnp.sum(jnp.where(taken, squares[None, None, :], 0.0), axis=2)
    rows = jnp.concatenate([packed, as_rows(squares, feat)], axis=1)
    rows = jnp.broadcast_to(rows[:, None], (EXPERTS, 2) + rows.shape[1:]).reshape(sources, CAP + 8, feat)
    rows = all_to_all(rows, GROUP)
    part_a, part_b = (rows[:, k * n : (k + 1) * n].reshape(block, feat) for k in range(2))
    x_a = along_z(part_a)
    squares = from_row(rows[:, CAP], CAP).reshape(sources, 2, n).transpose(1, 0, 2).reshape(2 * block)
    inverse = lax.rsqrt(lax.psum(squares, EXP) / D + 1e-05)
    inverse, w_gate, w_up = lax.optimization_barrier((inverse, w_gate, w_up))
    x_a, w_in, w_in_other = lax.optimization_barrier((x_a,) + prepare(w_gate, w_up))
    x_b = along_z(jnp.concatenate([part_b, as_rows(inverse, feat)], axis=0))

    def over_yl(parts):
        return [parts[0]] + [lax.ppermute(parts[i], "yl", Y_XOR[i]) for i in range(1, 4)]

    def hidden_of(parts, inverse):
        inverse = lax.dynamic_index_in_dim(inverse.reshape(4, -1), me, 0, keepdims=False)
        full = sum(p.astype(F32) for p in parts) * inverse[:, None]
        return (jax.nn.silu(full[:, :half]) * full[:, half:]).astype(BF16)

    def down_of(parts):
        hid = jnp.concatenate(parts, axis=0)
        return down_terms(order, hid, swap(hid, "c"), w_down)

    def give_back(down):
        return all_to_all(down.reshape(nz, block, feat), "z")

    def over_z(back):
        return jnp.sum(back.astype(F32), axis=0).astype(BF16).reshape(sources, n, feat)

    terms_a = gate_up_terms(order, x_a, swap(x_a, "c"), w_in, w_in_other, block)
    sums_a = over_yl(terms_a)
    x_b = after(x_b, sums_a[3])
    inverse = from_row(x_b[:, block], 2 * block)
    terms_b = gate_up_terms(order, x_b, swap(x_b, "c"), w_in, w_in_other, block)
    sums_a[1] = after(sums_a[1], *terms_b)
    hids_a = over_yl([hidden_of(sums_a, inverse[:, :block])] * 4)
    sums_b = over_yl(terms_b)
    hids_a[1] = after(hids_a[1], *sums_b[2:])
    down_a = down_of(hids_a)
    back_a = give_back(down_a)
    sums_b[1] = after(sums_b[1], down_a)
    hids_b = over_yl([hidden_of(sums_b, inverse[:, block:])] * 4)
    back_a = after(back_a, *hids_b[1:])
    back_b = give_back(down_of(hids_b))
    returned = all_to_all(jnp.concatenate([over_z(back_a), over_z(back_b)], axis=1), GROUP)
    returned = jnp.sum(returned.reshape(EXPERTS, 2, CAP, feat).astype(F32), axis=1)
    moe_rows = jnp.einsum(
        "ect,ecd->td", taken.astype(F32), returned, precision=lax.Precision.HIGHEST, preferred_element_type=F32
    )
    return (route_weight[:, None] * moe_rows).astype(BF16)


def solution(mesh):
    fine = Mesh(mesh.devices.reshape(2, 2, 2, 8, 4, 2), CTX + EXP)
    wide = P(CTX, EXP)
    in_specs = (wide, wide, wide, wide, P(EXP), P(CTX, None), P(CTX), wide, wide, wide)
    return jax.shard_map(body, mesh=fine, in_specs=in_specs, out_specs=wide, check_vma=False)
```
